32 devices in a mesh: dp: 8 (over z, x), tensor: 4 (over y, core).
Axes of the slice: x: 2, y: 2, z: 4, core: 2. Of those that a mesh axis runs over, the one named last changes fastest.
Arguments:
- patches: bfloat16 [192, 196, 768], P('dp'), may hold values from -6 to 6
- keep_slots: int32 [192, 98], P('dp'), may hold values from 0 to 195, as said below
- visible_count: int32 [192], P('dp'), may hold values from 39 to 98, as said below
- gain_one: float32 [768], replicated, may hold values from 0.1 to 1.9
- shift_one: float32 [768], replicated, may hold values from -4 to 4
- w_qkv: bfloat16 [3, 768, 768], P(None, None, 'tensor'), may hold values from -0.21875 to 0.21875
- b_qv: float32 [2, 768], P(None, 'tensor'), may hold values from -4 to 4
- w_out: bfloat16 [768, 768], P('tensor'), may hold values from -1.75 to 1.75
- b_out: float32 [768], replicated, may hold values from -4 to 4
- gain_two: float32 [768], replicated, may hold values from 0.1 to 1.9
- shift_two: float32 [768], replicated, may hold values from -4 to 4
- w_fc1: bfloat16 [768, 3072], P(None, 'tensor'), may hold values from -0.21875 to 0.21875
- b_fc1: float32 [3072], P('tensor'), may hold values from -4 to 4
- w_fc2: bfloat16 [3072, 768], P('tensor'), may hold values from -0.109375 to 0.109375
- b_fc2: float32 [768], replicated, may hold values from -4 to 4
- out_grad: bfloat16 [192, 98, 768], P(('dp', 'tensor')), may hold values from -6 to 6
Outputs:
- layer_out: bfloat16 [192, 98, 768], P(('dp', 'tensor'))
- grad_patches: float32 [192, 196, 768], P(('dp', 'tensor'))
- grad_gain_one: float32 [768], replicated
- grad_shift_one: float32 [768], replicated
- grad_w_qkv: float32 [3, 768, 768], P(None, None, 'tensor')
- grad_b_qv: float32 [2, 768], P(None, 'tensor')
- grad_w_out: float32 [768, 768], P('tensor')
- grad_b_out: float32 [768], replicated
- grad_gain_two: float32 [768], replicated
- grad_shift_two: float32 [768], replicated
- grad_w_fc1: float32 [768, 3072], P(None, 'tensor')
- grad_b_fc1: float32 [3072], P('tensor')
- grad_w_fc2: float32 [3072, 768], P('tensor')
- grad_b_fc2: float32 [768], replicated
The draws below stay inside these ranges and needn't reach their ends.
Inputs may be any that keep to these rules, and one draw needn't show every extreme that they name: `visible_count`: visible patches of each image; in every draw some image has 98 and some has 196 // 5. `keep_slots`: the entries of a row are distinct patch indices of the image; the first visible_count of them are its visible patches, the others are ignored.
All inputs are finite; a program needn't handle non-finite values.
Results may differ from the reference program's by a relative error of at most 0.012.
The reference program's roundings to bfloat16 on the way count: a program that leaves them out, or rounds other values in their place, can miss the bound.
Values may be sent and summed in bfloat16 or wider, within the bound.
No kernel may reach another device: no remote copies, remote signals or barrier semaphores. Data moves between devices by JAX's collectives and lax.ppermute only.
A program may use at most 192 MiB of HBM per device.

```python
import jax
import jax.numpy as jnp
from jax import lax

D = 768
H = 12
HD = 64
FF = 3072
P_SIZE = 196
IMG_DEV = 24
VMAX = 98
IMAGES = 192
N_DP = 8


def draw_visible_count(key, part):
    levels = jax.random.randint(key, (IMAGES,), P_SIZE // 5, P_SIZE // 2 + 1)
    places = jax.random.permutation(jax.random.fold_in(key, 3), IMAGES)
    levels = levels.at[places[0]].set(P_SIZE // 2)
    levels = levels.at[places[1]].set(P_SIZE // 5)
    return levels.astype(jnp.int32)


def draw_keep_slots(key, part):
    image_keys = jax.random.split(jax.random.fold_in(key, 11), IMAGES)
    orders = jax.vmap(lambda one_key: jax.random.permutation(one_key, P_SIZE))(image_keys)
    return orders[:, :P_SIZE // 2].astype(jnp.int32)


def block_levels(own_key, shape, cuts, smallest, high):
    factor_of, own = 1.0, jax.random.fold_in(own_key, 6)
    for dim, blocks in cuts:
        heights = jnp.exp(jax.random.uniform(jax.random.fold_in(own, dim), (blocks,), jnp.float32, smallest / len(cuts), high / len(cuts)))
        factor_of = factor_of * jnp.repeat(heights, shape[dim] // blocks).reshape([-1 if axis == dim else 1 for axis in range(len(shape))])
    return factor_of


def normal_values(key, dims, deviation, limit, cuts=(), kind=jnp.bfloat16):
    array = deviation * jax.random.normal(key, dims, jnp.float32)
    if cuts:
        array = array * block_levels(key, dims, cuts, -0.22, 0.18)
    return jnp.clip(array, -limit, limit).astype(kind)


def setup_inputs(seed: int = 0) -> dict:
    keys = jax.random.split(jax.random.key(seed), 17)
    patches = normal_values(keys[0], (IMAGES, P_SIZE, D), 1.0, 6.0, ((0, 8),))
    keep_slots = draw_keep_slots(jax.random.fold_in(keys[16], 71), 0)
    visible_count = draw_visible_count(jax.random.fold_in(keys[16], 71), 0)
    gain_one = jnp.clip(1.0 + 0.18 * jax.random.normal(keys[3], (D,), jnp.float32), 0.1, 1.9)
    shift_one = normal_values(keys[4], (D,), 0.3, 4.0, (), jnp.float32)
    w_qkv = normal_values(keys[5], (3, D, D), D ** -0.5, 0.21875, ((2, 4),))
    b_qv = normal_values(keys[6], (2, D), 0.5, 4.0, ((1, 4),), jnp.float32)
    w_out = normal_values(keys[7], (D, D), (max(D // 64, 1)) ** -0.5, 1.75, ((0, 4),))
    b_out = normal_values(keys[8], (D,), 0.5, 4.0, (), jnp.float32)
    gain_two = jnp.clip(1.0 + 0.18 * jax.random.normal(keys[9], (D,), jnp.float32), 0.1, 1.9)
    shift_two = normal_values(keys[10], (D,), 0.3, 4.0, (), jnp.float32)
    w_fc1 = normal_values(keys[11], (D, FF), D ** -0.5, 0.21875, ((1, 4),))
    b_fc1 = normal_values(keys[12], (FF,), 0.5, 4.0, ((0, 4),), jnp.float32)
    w_fc2 = normal_values(keys[13], (FF, D), FF ** -0.5, 0.109375, ((0, 4),))
    b_fc2 = normal_values(keys[14], (D,), 0.5, 4.0, (), jnp.float32)
    out_grad = normal_values(keys[15], (IMAGES, VMAX, D), 1.0, 6.0, ((0, 32),))
    return dict(patches=patches, keep_slots=keep_slots, visible_count=visible_count, gain_one=gain_one, shift_one=shift_one, w_qkv=w_qkv, b_qv=b_qv, w_out=w_out, b_out=b_out, gain_two=gain_two, shift_two=shift_two, w_fc1=w_fc1, b_fc1=b_fc1, w_fc2=w_fc2, b_fc2=b_fc2, out_grad=out_grad)


EPSILON = 1e-06
MASKED = -1000000000.0
HIGHEST = lax.Precision.HIGHEST

@jax.custom_vjp
def low(v):
    return lax.optimization_barrier(v.astype(jnp.bfloat16)).astype(jnp.float32)

@jax.custom_vjp
def low_back(v):
    return v

def low_keep(v):
    return (low(v), None)

def low_pass(kept, grad):
    return (grad,)

def back_keep(v):
    return (v, None)

def back_low(kept, grad):
    return (low(grad),)
low.defvjp(low_keep, low_pass)
low_back.defvjp(back_keep, back_low)

def rounded(values):
    return low_back(low(values))

def layer_norm(inputs, weights, offsets):
    average = lax.optimization_barrier(jnp.mean(inputs, axis=-1, keepdims=True))
    centered = inputs - average
    spread = lax.optimization_barrier(jnp.mean(centered * centered, axis=-1, keepdims=True))
    return centered * lax.rsqrt(spread + EPSILON) * weights + offsets

def product(left_side, right_side, pattern):
    return jnp.einsum(pattern, left_side, right_side, precision=HIGHEST)

def group_layer(params, patch_group, slot_group, count_group):
    gain_one, shift_one, w_qkv, b_qv, w_out, b_out, gain_two, shift_two, w_fc1, b_fc1, w_fc2, b_fc2 = params
    tokens = jnp.take_along_axis(patch_group, slot_group[:, :, None], axis=1)
    images, slots = slot_group.shape
    visible = jnp.arange(slots, dtype=jnp.int32)[None, :] < count_group[:, None]
    first = low(layer_norm(tokens, gain_one, shift_one))
    projected = product(first, w_qkv, 'ivd,sdh->sivh')
    heads_shape = (images, slots, H, HD)
    queries = rounded(projected[0] + b_qv[0]).reshape(heads_shape)
    keyset = rounded(projected[1]).reshape(heads_shape)
    valueset = rounded(projected[2] + b_qv[1]).reshape(heads_shape)
    scores = low_back(product(queries, keyset, 'iqhe,ikhe->ihqk') * HD ** (-0.5))
    scores = jnp.where(visible[:, None, None, :], scores, MASKED)
    highest = lax.optimization_barrier(jnp.max(scores, axis=-1, keepdims=True))
    logsum = highest + jnp.log(lax.optimization_barrier(jnp.sum(jnp.exp(scores - highest), axis=-1, keepdims=True)))
    attention = low(jnp.exp(scores - logsum))
    attended = rounded(product(attention, valueset, 'ihqk,ikhe->iqhe')).reshape(images, slots, H * HD)
    middle = tokens + low_back(product(attended, w_out, 'ivc,cd->ivd')) + b_out
    second = low(layer_norm(middle, gain_two, shift_two))
    inner = low_back(product(second, w_fc1, 'ivd,df->ivf') + b_fc1)
    hidden = low(jax.nn.gelu(inner, approximate=False))
    branch_two = low_back(product(hidden, w_fc2, 'ivf,fd->ivd'))
    return (middle + branch_two + b_fc2) * visible[:, :, None].astype(jnp.float32)

def reference(patches, keep_slots, visible_count, gain_one, shift_one, w_qkv, b_qv, w_out, b_out, gain_two, shift_two, w_fc1, b_fc1, w_fc2, b_fc2, out_grad):
    params = tuple((argument.astype(jnp.float32) for argument in (gain_one, shift_one, w_qkv, b_qv, w_out, b_out, gain_two, shift_two, w_fc1, b_fc1, w_fc2, b_fc2)))

    def forward(weights_all, patch_values):
        patch_blocks = patch_values.reshape(N_DP, IMG_DEV, P_SIZE, D)
        slot_blocks = keep_slots.reshape(N_DP, IMG_DEV, VMAX)
        count_blocks = visible_count.reshape(N_DP, IMG_DEV)

        def one_block(block):
            return group_layer(weights_all, block[0], block[1], block[2])
        results = lax.map(jax.checkpoint(one_block), (patch_blocks, slot_blocks, count_blocks))
        return results.reshape(IMAGES, VMAX, D)
    layer_out, backward = jax.vjp(forward, params, patches.astype(jnp.float32))
    grad_params, grad_patches = backward(out_grad.astype(jnp.float32))
    grad_gain_one, grad_shift_one, grad_w_qkv, grad_b_qv, grad_w_out, grad_b_out, grad_gain_two, grad_shift_two, grad_w_fc1, grad_b_fc1, grad_w_fc2, grad_b_fc2 = grad_params
    return (layer_out.astype(jnp.bfloat16), grad_patches, grad_gain_one, grad_shift_one, grad_w_qkv, grad_b_qv, grad_w_out, grad_b_out, grad_gain_two, grad_shift_two, grad_w_fc1, grad_b_fc1, grad_w_fc2, grad_b_fc2)
```

```python
import functools

import jax
import jax.numpy as jnp
from jax import lax
from jax.experimental import pallas as pl
from jax.experimental.pallas import tpu as pltpu
from jax.sharding import PartitionSpec as P

HD = 64
EPSILON = 1e-06
MASKED = -1000000000.0
F32 = jnp.float32
BF16 = jnp.bfloat16
VMEM = pltpu.VMEM
NN = (((1,), (0,)), ((), ()))
NT = (((1,), (1,)), ((), ()))
TN = (((0,), (0,)), ((), ()))


def dot(left, right, dims=NN):
    return lax.dot_general(left, right, dims, preferred_element_type=F32)


def standard(inputs):
    average = jnp.mean(inputs, axis=-1, keepdims=True)
    centered = inputs - average
    spread = jnp.mean(centered * centered, axis=-1, keepdims=True)
    inverse = lax.rsqrt(spread + EPSILON)
    return centered * inverse, inverse


def norm_back(normal, inverse, gain, gradient):
    scaled = gradient * gain
    first = jnp.mean(scaled, axis=-1, keepdims=True)
    second = jnp.mean(scaled * normal, axis=-1, keepdims=True)
    return inverse * (scaled - first - normal * second)


def slots_matrix(keep_row, patch_count):
    places = lax.broadcasted_iota(jnp.int32, (patch_count, keep_row.shape[1]), 0)
    return (places == keep_row).astype(F32).astype(BF16)


def add_row(ref, value):
    row = jnp.sum(value, axis=0, keepdims=True)

    @pl.when(pl.program_id(0) == 0)
    def _():
        ref[...] = jnp.zeros_like(ref)

    ref[...] += row


def full(shape):
    return pl.BlockSpec(shape, lambda i, *_: (0,) * len(shape))


def rows(count, width):
    return pl.BlockSpec((count, width), lambda i, *_: (i, 0))


def call(body, grid, scalars, ins, in_specs, outs, out_specs, scratch=(), flops=0, alias=None):
    size = sum(a.size * a.dtype.itemsize for a in ins)
    size += sum(o.size * o.dtype.itemsize for o in outs)
    return pl.pallas_call(
        body,
        out_shape=outs,
        grid_spec=pltpu.PrefetchScalarGridSpec(
            num_scalar_prefetch=len(scalars),
            grid=grid,
            in_specs=in_specs,
            out_specs=out_specs,
            scratch_shapes=scratch,
        ),
        compiler_params=pltpu.CompilerParams(vmem_limit_bytes=50 * 2**20),
        input_output_aliases=alias or {},
        cost_estimate=pl.CostEstimate(flops=100 * flops, bytes_accessed=100 * size, transcendentals=0),
    )(*scalars, *ins)


def shape_of(shape, kind):
    return jax.ShapeDtypeStruct(shape, kind)


def prepare(place, counts, keep, patches, out_grad, gain, shift, slots):
    share, padded, width = out_grad.shape[0], keep.shape[1], patches.shape[2]
    patch_count = patches.shape[1]
    total = share * padded

    def body(place_ref, count_ref, keep_ref, patch_ref, grad_ref, gain_ref, shift_ref, *outs):
        tokens_ref, first_ref, rows_ref, sum_ref = outs
        image = place_ref[0] + pl.program_id(0)
        picks = slots_matrix(keep_ref[pl.ds(image, 1), :], patch_count)
        tokens = dot(picks, patch_ref[0], TN)
        tokens_ref[...] = tokens.astype(BF16)
        normal, _ = standard(tokens)
        first_ref[...] = (normal * gain_ref[...] + shift_ref[...]).astype(BF16)
        seen = lax.broadcasted_iota(jnp.int32, (slots, 1), 0) < count_ref[image]
        grads = jnp.where(seen, grad_ref[0].astype(F32), 0.0)
        rows_ref[...] = jnp.zeros_like(rows_ref)
        rows_ref[0:slots, :] = grads.astype(BF16)
        add_row(sum_ref, grads)

    return call(
        body,
        (share,),
        (place, counts),
        (keep, patches, out_grad, gain, shift),
        [
            full(keep.shape),
            pl.BlockSpec((1, patch_count, width), lambda i, p, c: (p[0] + i, 0, 0)),
            pl.BlockSpec((1, slots, width), lambda i, *_: (i, 0, 0)),
            full(gain.shape),
            full(shift.shape),
        ],
        (shape_of((total, width), BF16),) * 3 + (shape_of((1, width), F32),),
        [rows(padded, width)] * 3 + [full((1, width))],
        flops=2 * total * patch_count * width,
    )


def heads_of(width):
    lanes = lax.broadcasted_iota(jnp.int32, (1, width), 1) // HD
    return [(lanes == h).astype(BF16) for h in range(width // HD)]


def stacked(values, masks):
    return jnp.concatenate([values * m for m in masks], axis=0)


def merged(values, masks, length):
    lanes = lax.broadcasted_iota(jnp.int32, (1, values.shape[1]), 1) // HD
    result = values[0:length]
    for h in range(1, len(masks)):
        result = jnp.where(lanes == h, values[h * length : (h + 1) * length], result)
    return result


def probabilities(queries, keys, count, masks):
    scores = dot(stacked(queries, masks), keys, NT) * HD**-0.5
    seen = lax.broadcasted_iota(jnp.int32, (1, keys.shape[0]), 1) < count
    scores = jnp.where(seen, scores, MASKED)
    powers = jnp.exp(scores - jnp.max(scores, axis=-1, keepdims=True))
    return powers / jnp.sum(powers, axis=-1, keepdims=True)


def attend(place, counts, first, weights, bias, padded):
    total, width = first.shape
    inner = bias.shape[1]
    part = inner // 3
    group = 2

    def body(place_ref, count_ref, first_ref, w_ref, bias_ref, qkv_ref, out_ref):
        masks = heads_of(part)
        qkv = dot(first_ref[...], w_ref[...], NT) + bias_ref[...]
        qkv = qkv.astype(BF16)
        qkv_ref[...] = qkv
        for g in range(group):
            image = place_ref[0] + pl.program_id(0) * group + g
            block = qkv[g * padded : (g + 1) * padded]
            q, k, v = (block[:, j * part : (j + 1) * part] for j in range(3))
            chances = probabilities(q, k, count_ref[image], masks).astype(BF16)
            mixed = dot(chances, v)
            out_ref[g * padded : (g + 1) * padded, :] = merged(mixed, masks, padded).astype(BF16)

    size = group * padded
    return call(
        body,
        (total // size,),
        (place, counts),
        (first, weights, bias),
        [rows(size, width), full((inner, width)), full(bias.shape)],
        (shape_of((total, inner), BF16), shape_of((total, part), BF16)),
        [rows(size, inner), rows(size, part)],
        flops=2 * total * inner * width,
    )


def join(tokens, attended, weights, b_out, gain, shift, size):
    total, width = tokens.shape
    part = attended[0].shape[1]
    n = len(attended)

    def body(*refs):
        tokens_ref, refs = refs[0], refs[1:]
        att_refs, w_refs = refs[:n], refs[n : 2 * n]
        bias_ref, gain_ref, shift_ref, middle_ref, second_ref = refs[2 * n :]
        middle = tokens_ref[...].astype(F32) + bias_ref[...]
        branch = dot(att_refs[0][...], w_refs[0][...])
        for a, w in zip(att_refs[1:], w_refs[1:]):
            branch += dot(a[...], w[...])
        middle += branch
        middle_ref[...] = middle
        normal, _ = standard(middle)
        second_ref[...] = (normal * gain_ref[...] + shift_ref[...]).astype(BF16)

    last = width // part - 1
    return call(
        body,
        (total // size,),
        (),
        (tokens, *attended, *weights, b_out, gain, shift),
        [rows(size, width)]
        + [rows(size, part)] * n
        + [pl.BlockSpec((part, width), lambda i: (last, 0))] * n
        + [full((1, width))] * 3,
        (shape_of((total, width), F32), shape_of((total, width), BF16)),
        [rows(size, width)] * 2,
        flops=2 * total * width * width,
    )


def feed(second, grads, up, down, bias, before, size):
    total, width = second.shape
    units = up.shape[1]
    steps = total // size
    root = 0.5**0.5
    density = (2.0 * jnp.pi) ** -0.5

    def body(*refs):
        second_ref, grads_ref, up_ref, down_ref, bias_ref = refs[:5]
        refs = refs[5:]
        if before:
            out_before, back_before = refs[:2]
            refs = refs[2:]
        out_ref, back_ref, d_up_ref, d_down_ref, d_bias_ref, hidden_ref, inner_ref = refs
        for s in range(steps):
            here = slice(s * size, (s + 1) * size)
            u = dot(second_ref[here, :], up_ref[...]) + bias_ref[...]
            gh = dot(grads_ref[here, :], down_ref[...], NT)
            below = 0.5 + 0.5 * lax.erf(u * root)
            hidden = (u * below).astype(BF16)
            slope = below + u * (jnp.exp(-0.5 * u * u) * density)
            gi = (gh * slope).astype(BF16)
            hidden_ref[here, :] = hidden
            inner_ref[here, :] = gi
            row = jnp.sum(gi.astype(F32), axis=0, keepdims=True)
            d_bias_ref[...] = row if s == 0 else d_bias_ref[...] + row
            out = dot(hidden, down_ref[...])
            back = dot(gi, up_ref[...], NT)
            if before:
                out += out_before[here, :]
                back += back_before[here, :]
            out_ref[here, :] = out
            back_ref[here, :] = back
        d_down_ref[...] = dot(hidden_ref[...], grads_ref[...], TN).astype(BF16)
        d_up_ref[...] = dot(second_ref[...], inner_ref[...], TN).astype(BF16)

    ins = (second, grads, up, down, bias, *before)
    outs = (
        shape_of((total, width), F32),
        shape_of((total, width), F32),
        shape_of((width, units), BF16),
        shape_of((units, width), BF16),
        shape_of((1, units), F32),
    )
    return call(
        body,
        (1,),
        (),
        ins,
        [full(a.shape) for a in ins],
        outs,
        [full(o.shape) for o in outs],
        scratch=[VMEM((total, units), BF16), VMEM((total, units), BF16)],
        flops=12 * total * width * units,
        alias={5: 0, 6: 1} if before else None,
    )


def middle_back(place, counts, middle, back, grads, out, gain, b_fc2, padded, slots):
    total, width = middle.shape
    share = total // padded

    def body(place_ref, count_ref, middle_ref, back_ref, grads_ref, out_ref, gain_ref, bias_ref, *outs):
        grad_ref, round_ref, layer_ref, d_gain_ref, d_shift_ref, d_bias_ref = outs
        middle = middle_ref[...]
        back = back_ref[...]
        normal, inverse = standard(middle)
        grad = grads_ref[...].astype(F32) + norm_back(normal, inverse, gain_ref[...], back)
        grad_ref[...] = grad
        round_ref[...] = grad.astype(BF16)
        add_row(d_gain_ref, back * normal)
        add_row(d_shift_ref, back)
        add_row(d_bias_ref, grad)
        image = place_ref[0] + pl.program_id(0)
        layer = middle + out_ref[...] + bias_ref[...]
        seen = lax.broadcasted_iota(jnp.int32, (padded, 1), 0) < count_ref[image]
        layer_ref[0] = jnp.where(seen, layer, 0.0).astype(BF16)[0:slots]

    one = shape_of((1, width), F32)
    return call(
        body,
        (share,),
        (place, counts),
        (middle, back, grads, out, gain, b_fc2),
        [rows(padded, width)] * 4 + [full((1, width))] * 2,
        (
            shape_of((total, width), F32),
            shape_of((total, width), BF16),
            shape_of((share, slots, width), BF16),
            one,
            one,
            one,
        ),
        [rows(padded, width)] * 2
        + [pl.BlockSpec((1, slots, width), lambda i, *_: (i, 0, 0))]
        + [full((1, width))] * 3,
        flops=20 * total * width,
    )


def attend_back(place, counts, grad, weights, qkv, attended, first, before, padded):
    total, width = grad.shape
    inner, part = qkv.shape[1], attended.shape[1]
    share = total // padded

    def body(place_ref, count_ref, grad_ref, w_ref, qkv_ref, att_ref, first_ref, *refs):
        if before:
            before_ref, refs = refs[0], refs[1:]
        back_ref, d_w_ref, d_bias_ref, three_ref = refs
        masks = heads_of(part)
        for i in range(share):
            here = slice(i * padded, (i + 1) * padded)
            ga = dot(grad_ref[here, :], w_ref[inner:, :], NT).astype(BF16)
            q, k, v = (qkv_ref[here, j * part : (j + 1) * part] for j in range(3))
            exact = probabilities(q, k, count_ref[place_ref[0] + i], masks)
            ga_all = stacked(ga, masks)
            gp = dot(ga_all, v, NT)
            gs = exact * (gp - jnp.sum(exact * gp, axis=-1, keepdims=True))
            gs = gs.astype(BF16)
            gq = merged(dot(gs, k), masks, padded) * HD**-0.5
            gk = dot(gs, stacked(q, masks), TN) * HD**-0.5
            gv = dot(exact.astype(BF16), ga_all, TN)
            for j, value in enumerate((gq, gk, gv)):
                three_ref[here, j * part : (j + 1) * part] = value.astype(BF16)
            back = dot(three_ref[here, :], w_ref[:inner, :])
            if before:
                back += before_ref[here, :]
            back_ref[here, :] = back
        d_w_ref[:inner, :] = dot(three_ref[...], first_ref[...], TN).astype(BF16)
        d_w_ref[inner:, :] = dot(att_ref[...], grad_ref[...], TN).astype(BF16)
        d_bias_ref[...] = jnp.sum(three_ref[...].astype(F32), axis=0, keepdims=True)

    ins = (grad, weights, qkv, attended, first, *before)
    outs = (
        shape_of((total, width), F32),
        shape_of(weights.shape, BF16),
        shape_of((1, inner), F32),
    )
    return call(
        body,
        (1,),
        (place, counts),
        ins,
        [full(a.shape) for a in ins],
        outs,
        [full(o.shape) for o in outs],
        scratch=[VMEM((total, inner), BF16)],
        flops=6 * total * width * width,
        alias={7: 0} if before else None,
    )


def finish(place, keep, tokens, back, grad, gain, patch_count, padded):
    total, width = tokens.shape
    share = total // padded

    def body(place_ref, keep_ref, tokens_ref, back_ref, grad_ref, gain_ref, out_ref, d_gain_ref, d_shift_ref):
        back = back_ref[...]
        normal, inverse = standard(tokens_ref[...].astype(F32))
        grad = grad_ref[...] + norm_back(normal, inverse, gain_ref[...], back)
        add_row(d_gain_ref, back * normal)
        add_row(d_shift_ref, back)
        image = place_ref[0] + pl.program_id(0)
        picks = slots_matrix(keep_ref[pl.ds(image, 1), :], patch_count)
        high = grad.astype(BF16)
        low = (grad - high.astype(F32)).astype(BF16)
        out_ref[0] = dot(picks, high) + dot(picks, low)

    one = shape_of((1, width), F32)
    return call(
        body,
        (share,),
        (place,),
        (keep, tokens, back, grad, gain),
        [full(keep.shape)] + [rows(padded, width)] * 3 + [full((1, width))],
        (shape_of((share, patch_count, width), F32), one, one),
        [pl.BlockSpec((1, patch_count, width), lambda i, *_: (i, 0, 0))] + [full((1, width))] * 2,
        flops=4 * total * patch_count * width,
    )


def swap(value, axis, bit):
    size = lax.axis_size(axis)
    return lax.ppermute(value, axis, [(i, i ^ bit) for i in range(size)])


def after(value, *others):
    return lax.optimization_barrier((value, *others))[0]


def half(value, bit):
    size = value.shape[0] // 2
    return lax.dynamic_slice_in_dim(value, bit * size, size, 0)


def whole(mine, other, bit):
    return jnp.where(
        bit == 0, jnp.concatenate([mine, other], axis=0), jnp.concatenate([other, mine], axis=0)
    )


def place_bit(bit):
    return (lax.axis_index("dp") // bit) % 2


class Images:
    def __init__(self, value):
        self.value = value
        size = lax.axis_size("dp")
        bits = []
        while 2 ** len(bits) < size:
            bits.append(2 ** len(bits))
        self.steps = [("sum", bit) for bit in bits] + [("join", bit) for bit in reversed(bits)]
        self.sent = None
        self.start()

    def start(self):
        if not self.steps:
            return
        kind, bit = self.steps[0]
        if kind == "sum":
            outgoing = half(self.value, 1 - place_bit(bit)).astype(BF16)
            self.value = half(self.value, place_bit(bit))
        else:
            outgoing = self.value = self.value.astype(BF16)
        self.sent = swap(outgoing, "dp", bit)
        self.ready = outgoing

    def step(self, *others):
        if not self.steps:
            return self.value
        kind, bit = self.steps.pop(0)
        arrived = after(self.sent, *others) if others else self.sent
        if kind == "sum":
            self.value = self.value.astype(F32) + arrived.astype(F32)
        else:
            self.value = whole(self.value, arrived, place_bit(bit))
        self.start()
        return self.ready if self.steps else self.value

    def finish(self):
        while self.steps:
            self.step()
        return self.value.astype(F32)


def reduce_all(value):
    for axis in ("tensor", "dp"):
        bit = 1
        while bit < lax.axis_size(axis):
            value = value + swap(value, axis, bit)
            bit *= 2
    return value


def shards(
    patches,
    keep_slots,
    visible_count,
    gain_one,
    shift_one,
    w_qkv,
    b_qv,
    w_out,
    b_out,
    gain_two,
    shift_two,
    w_fc1,
    b_fc1,
    w_fc2,
    b_fc2,
    out_grad,
):
    images, slots = keep_slots.shape
    patch_count, width = patches.shape[1:]
    tensor = lax.axis_size("tensor")
    spot = lax.axis_index("tensor")
    share = images // tensor
    padded = -(-slots // 8) * 8
    part, units = w_qkv.shape[2], w_fc1.shape[1]
    inner = 3 * part
    begin = spot * share
    place = jnp.zeros((1,), jnp.int32)
    counts = lax.dynamic_slice_in_dim(visible_count, begin, share, 0)
    keep = lax.dynamic_slice_in_dim(keep_slots, begin, share, 0)
    keep = jnp.pad(keep, ((0, 0), (0, padded - slots)), constant_values=-1)
    patches = lax.dynamic_slice_in_dim(patches, begin, share, 0)
    line = lambda vector: vector.reshape(1, -1)
    side = place_bit(1)

    own = jnp.concatenate([w_qkv.transpose(0, 2, 1).reshape(inner, width), w_out], axis=0)
    far_mix = swap(half(own, side), "tensor", 2)
    near_mix = swap(own, "tensor", 1)
    biases = line(jnp.concatenate([b_qv[0], jnp.zeros_like(b_qv[0]), b_qv[1], b_fc1]))
    biases = jnp.concatenate([biases, swap(biases, "tensor", 1)], axis=0)
    biases = jnp.concatenate([biases, swap(biases, "tensor", 2)], axis=0)
    biases = [biases[r : r + 1] for r in range(tensor)]

    tokens, first, grad_rows, g_b_fc2 = prepare(
        place, counts, keep, patches, out_grad, line(gain_one), line(shift_one), slots
    )
    three, attended = [None] * 4, [None] * 4

    def attending(r, weights, *others):
        three[r], attended[r] = attend(
            place, counts, after(first, *others), weights, biases[r][:, :inner], padded
        )
        return attended[r]

    far_down = swap(half(after(w_fc2, first), side), "tensor", 2)
    done = attending(0, own)
    far_up = swap(after(w_fc1, done), "tensor", 2)
    done = attending(1, near_mix, done)
    far_mix = after(far_mix, done)
    far_mix = whole(far_mix, swap(far_mix, "dp", 1), side)
    cross_mix = swap(far_mix, "tensor", 1)
    done = attending(2, far_mix, done)
    done = attending(3, cross_mix, done)
    mixes = [own, near_mix, far_mix, cross_mix]
    far_down = after(far_down, done)
    far_down_other = swap(far_down, "dp", 1)
    near_up, near_down = (swap(after(w, done), "tensor", 1) for w in (w_fc1, w_fc2))
    middle, second = join(
        tokens, attended, mixes, line(b_out), line(gain_two), line(shift_two), 2 * padded
    )
    g_up, g_down, g_b_fc1 = [None] * 4, [None] * 4, [None] * 4
    before = ()

    def feeding(r, up, down, before, *others):
        out, back, g_up[r], g_down[r], g_b_fc1[r] = feed(
            after(second, *others), grad_rows, up, down, biases[r][:, inner:], before, 2 * padded
        )
        return out, back

    before = feeding(0, w_fc1, w_fc2, before)
    far_up = after(far_up, before[0])
    far_down = whole(far_down, after(far_down_other, before[0]), side)
    cross_up, cross_down = swap(far_up, "tensor", 1), swap(far_down, "tensor", 1)
    before = feeding(2, far_up, far_down, before)
    before = feeding(3, cross_up, cross_down, before)
    ends = [swap(g[3], "tensor", 1) for g in (g_up, g_down)]
    before = feeding(1, near_up, near_down, before)
    fars = [(g[2].astype(F32) + after(e, before[0]).astype(F32)).astype(BF16) for g, e in zip((g_up, g_down), ends)]
    fars = [swap(f, "tensor", 2) for f in fars]
    nears = [swap(g[1], "tensor", 1) for g in (g_up, g_down)]
    out, back = before
    grad_middle, grad_round, layer_out, g_gain_two, g_shift_two, g_b_out = middle_back(
        place, counts, middle, back, grad_rows, out, line(gain_two), line(b_fc2), padded, slots
    )
    g_mix, g_b_qkv = [None] * 4, [None] * 4

    def attending_back(r, before, *others):
        back, g_mix[r], g_b_qkv[r] = attend_back(
            place, counts, after(grad_round, *others), mixes[r], three[r], attended[r], first, before, padded
        )
        return (back,)

    before = attending_back(3, ())
    end = swap(g_mix[3], "tensor", 1)
    mine = [g[0].astype(F32) + n.astype(F32) for g, n in zip((g_up, g_down), nears)]
    one = Images(mine[0] + after(fars[0], before[0]).astype(F32))
    before = attending_back(2, before, one.ready)
    far = swap((g_mix[2].astype(F32) + after(end, before[0]).astype(F32)).astype(BF16), "tensor", 2)
    before = attending_back(1, before, one.step(before[0]))
    near = swap(g_mix[1], "tensor", 1)
    two = Images(mine[1] + after(fars[1], before[0]).astype(F32))
    before = attending_back(0, before, one.step(before[0]), two.ready)
    (back,) = before
    grad_patches, g_gain_one, g_shift_one = finish(
        place, keep, tokens, after(back, one.step(back), two.step(back)), grad_middle, line(gain_one), patch_count, padded
    )
    three = Images(g_mix[0].astype(F32) + near.astype(F32) + far.astype(F32))
    grad_w_fc1, grad_w_fc2, grad_mix = one.finish(), two.finish(), three.finish()
    shared = jnp.concatenate([g_gain_one, g_shift_one, g_b_out, g_gain_two, g_shift_two, g_b_fc2])
    local = jnp.concatenate([jnp.concatenate(g_b_qkv), jnp.concatenate(g_b_fc1)], axis=1)
    order = [lax.dynamic_slice_in_dim(local, spot ^ r, 1, 0) for r in range(tensor)]
    small = jnp.concatenate([shared.reshape(1, -1), jnp.concatenate(order, axis=0).reshape(1, -1)], axis=1)
    small = reduce_all(small)
    shared = small[0, : 6 * width].reshape(6, width)
    local = small[:, 6 * width :].reshape(tensor, inner + units)
    local = lax.dynamic_slice_in_dim(local, spot, 1, 0)[0]
    grad_b_qv = jnp.stack([local[:part], local[2 * part : inner]])
    grad_w_qkv = grad_mix[:inner].reshape(3, part, width).transpose(0, 2, 1)
    return (
        layer_out,
        grad_patches,
        shared[0],
        shared[1],
        grad_w_qkv,
        grad_b_qv,
        grad_mix[inner:],
        shared[2],
        shared[3],
        shared[4],
        grad_w_fc1,
        local[inner:],
        grad_w_fc2,
        shared[5],
    )


def solution(mesh):
    return jax.shard_map(
        shards,
        mesh=mesh,
        in_specs=(
            P("dp", None, None),
            P("dp", None),
            P("dp"),
            P(),
            P(),
            P(None, None, "tensor"),
            P(None, "tensor"),
            P("tensor", None),
            P(),
            P(),
            P(),
            P(None, "tensor"),
            P("tensor"),
            P("tensor", None),
            P(),
            P(("dp", "tensor"), None, None),
        ),
        out_specs=(
            P(("dp", "tensor"), None, None),
            P(("dp", "tensor"), None, None),
            P(),
            P(),
            P(None, None, "tensor"),
            P(None, "tensor"),
            P("tensor", None),
            P(),
            P(),
            P(),
            P(None, "tensor"),
            P("tensor"),
            P("tensor", None),
            P(),
        ),
        check_vma=False,
    )
```

```python
import functools

import jax
import jax.numpy as jnp
from jax import lax
from jax.experimental import pallas as pl
from jax.experimental.pallas import tpu as pltpu
from jax.sharding import PartitionSpec as P

HD = 64
EPSILON = 1e-06
MASKED = -1000000000.0
F32 = jnp.float32
BF16 = jnp.bfloat16
VMEM = pltpu.VMEM
NN = (((1,), (0,)), ((), ()))
NT = (((1,), (1,)), ((), ()))
TN = (((0,), (0,)), ((), ()))


def dot(left, right, dims=NN):
    return lax.dot_general(left, right, dims, preferred_element_type=F32)


def standard(inputs):
    average = jnp.mean(inputs, axis=-1, keepdims=True)
    centered = inputs - average
    spread = jnp.mean(centered * centered, axis=-1, keepdims=True)
    inverse = lax.rsqrt(spread + EPSILON)
    return centered * inverse, inverse


def norm_back(normal, inverse, gain, gradient):
    scaled = gradient * gain
    first = jnp.mean(scaled, axis=-1, keepdims=True)
    second = jnp.mean(scaled * normal, axis=-1, keepdims=True)
    return inverse * (scaled - first - normal * second)


def slots_matrix(keep_row, patch_count):
    places = lax.broadcasted_iota(jnp.int32, (patch_count, keep_row.shape[1]), 0)
    return (places == keep_row).astype(F32).astype(BF16)


def add_row(ref, value):
    row = jnp.sum(value, axis=0, keepdims=True)

    @pl.when(pl.program_id(0) == 0)
    def _():
        ref[...] = jnp.zeros_like(ref)

    ref[...] += row


def full(shape):
    return pl.BlockSpec(shape, lambda i, *_: (0,) * len(shape))


def rows(count, width):
    return pl.BlockSpec((count, width), lambda i, *_: (i, 0))


def call(body, grid, scalars, ins, in_specs, outs, out_specs, scratch=(), flops=0, alias=None, limit=24):
    size = sum(a.size * a.dtype.itemsize for a in ins)
    size += sum(o.size * o.dtype.itemsize for o in outs)
    return pl.pallas_call(
        body,
        out_shape=outs,
        grid_spec=pltpu.PrefetchScalarGridSpec(
            num_scalar_prefetch=len(scalars),
            grid=grid,
            in_specs=in_specs,
            out_specs=out_specs,
            scratch_shapes=scratch,
        ),
        compiler_params=pltpu.CompilerParams(vmem_limit_bytes=limit * 2**20),
        input_output_aliases=alias or {},
        cost_estimate=pl.CostEstimate(flops=100 * flops, bytes_accessed=100 * size, transcendentals=0),
    )(*scalars, *ins)


def shape_of(shape, kind):
    return jax.ShapeDtypeStruct(shape, kind)


def heads_of(width):
    lanes = lax.broadcasted_iota(jnp.int32, (1, width), 1) // HD
    return [(lanes == h).astype(BF16) for h in range(width // HD)]


def stacked(values, masks):
    return jnp.concatenate([values * m for m in masks], axis=0)


def merged(values, masks, length):
    lanes = lax.broadcasted_iota(jnp.int32, (1, values.shape[1]), 1) // HD
    result = values[0:length]
    for h in range(1, len(masks)):
        result = jnp.where(lanes == h, values[h * length : (h + 1) * length], result)
    return result


def probabilities(queries, keys, count, masks):
    scores = dot(stacked(queries, masks), keys, NT) * HD**-0.5
    seen = lax.broadcasted_iota(jnp.int32, (1, keys.shape[0]), 1) < count
    scores = jnp.where(seen, scores, MASKED)
    powers = jnp.exp(scores - jnp.max(scores, axis=-1, keepdims=True))
    return powers / jnp.sum(powers, axis=-1, keepdims=True)


def attention(first, w_ref, count, masks, qkv_ref, out_ref, here):
    inner = qkv_ref.shape[1]
    part = inner // 3
    bias = jnp.sum(w_ref[inner + part :, :].astype(F32), axis=0, keepdims=True)[:, :inner]
    qkv = (dot(first, w_ref[:inner, :], NT) + bias).astype(BF16)
    qkv_ref[here, :] = qkv
    q, k, v = (qkv[:, j * part : (j + 1) * part] for j in range(3))
    chances = probabilities(q, k, count, masks).astype(BF16)
    mixed = merged(dot(chances, v), masks, first.shape[0]).astype(BF16)
    out_ref[here, :] = mixed


def begin(counts, keep, patches, out_grad, gain, shift, weights, inner):
    share, padded = keep.shape
    slots = out_grad.shape[1]
    patch_count, width = patches.shape[1:]
    total, n = share * padded, len(weights)
    part = inner // 3
    group = 2
    size = group * padded

    def body(count_ref, keep_ref, patch_ref, grad_ref, gain_ref, shift_ref, *refs):
        w_refs, outs = refs[:n], refs[n:]
        tokens_ref, first_ref, rows_ref, sum_ref = outs[:4]
        qkv_refs, att_refs = outs[4 : 4 + n], outs[4 + n :]
        masks = heads_of(part)
        total_sum = jnp.zeros((1, width), F32)
        for g in range(group):
            image = pl.program_id(0) * group + g
            here = slice(g * padded, (g + 1) * padded)
            picks = slots_matrix(keep_ref[pl.ds(image, 1), :], patch_count)
            tokens = dot(picks, patch_ref[g], TN)
            tokens_ref[here, :] = tokens.astype(BF16)
            normal, _ = standard(tokens)
            first = (normal * gain_ref[...] + shift_ref[...]).astype(BF16)
            first_ref[here, :] = first
            seen = lax.broadcasted_iota(jnp.int32, (slots, 1), 0) < count_ref[image]
            grads = jnp.where(seen, grad_ref[g].astype(F32), 0.0)
            rows_ref[here, :] = jnp.zeros((padded, width), BF16)
            rows_ref[g * padded : g * padded + slots, :] = grads.astype(BF16)
            total_sum += jnp.sum(grads, axis=0, keepdims=True)
            for w_ref, qkv_ref, att_ref in zip(w_refs, qkv_refs, att_refs):
                attention(first, w_ref, count_ref[image], masks, qkv_ref, att_ref, here)
        add_row(sum_ref, total_sum)

    return call(
        body,
        (share // group,),
        (counts,),
        (keep, patches, out_grad, gain, shift, *weights),
        [
            full(keep.shape),
            pl.BlockSpec((group, patch_count, width), lambda i, *_: (i, 0, 0)),
            pl.BlockSpec((group, slots, width), lambda i, *_: (i, 0, 0)),
            full(gain.shape),
            full(shift.shape),
        ]
        + [full(w.shape) for w in weights],
        (shape_of((total, width), BF16),) * 3
        + (shape_of((1, width), F32),)
        + (shape_of((total, inner), BF16),) * n
        + (shape_of((total, part), BF16),) * n,
        [rows(size, width)] * 3
        + [full((1, width))]
        + [rows(size, inner)] * n
        + [rows(size, part)] * n,
        flops=2 * total * (patch_count + n * inner) * width,
    )


def attend(counts, first, weights, padded, inner):
    total, width = first.shape
    n, part = len(weights), inner // 3
    group = 2
    size = group * padded

    def body(count_ref, first_ref, *refs):
        w_refs, qkv_refs, att_refs = refs[:n], refs[n : 2 * n], refs[2 * n :]
        masks = heads_of(part)
        for g in range(group):
            here = slice(g * padded, (g + 1) * padded)
            count = count_ref[pl.program_id(0) * group + g]
            for w_ref, qkv_ref, att_ref in zip(w_refs, qkv_refs, att_refs):
                attention(first_ref[here, :], w_ref, count, masks, qkv_ref, att_ref, here)

    return call(
        body,
        (total // size,),
        (counts,),
        (first, *weights),
        [rows(size, width)] + [full(w.shape) for w in weights],
        (shape_of((total, inner), BF16),) * n + (shape_of((total, part), BF16),) * n,
        [rows(size, inner)] * n + [rows(size, part)] * n,
        flops=2 * total * n * inner * width,
    )


def join(tokens, attended, w_outs, b_out, gain, shift, before, h):
    total, width = tokens.shape
    size, n = total // 2, len(attended)
    part = attended[0].shape[1]

    def body(tokens_ref, *refs):
        att_refs, o_refs, refs = refs[:n], refs[n : 2 * n], refs[2 * n :]
        bias_ref, gain_ref, shift_ref = refs[:3]
        middle_ref, second_ref = refs[3 + len(before) :]
        rows_of_out = slice(3 * part, 4 * part)
        branch = sum(dot(a[...], o[rows_of_out, :]) for a, o in zip(att_refs, o_refs))
        middle = tokens_ref[...].astype(F32) + branch + bias_ref[...]
        middle_ref[...] = middle
        normal, _ = standard(middle)
        second_ref[...] = (normal * gain_ref[...] + shift_ref[...]).astype(BF16)

    at = lambda wide: pl.BlockSpec((size, wide), lambda i: (h, 0))
    ins = (tokens, *attended, *w_outs, b_out, gain, shift)
    specs = [at(width)] + [at(part)] * n + [full(w.shape) for w in ins[1 + n :]]
    return call(
        body,
        (1,),
        (),
        ins + tuple(before),
        specs + [pl.BlockSpec(memory_space=pl.ANY)] * len(before),
        (shape_of((total, width), F32), shape_of((size, width), BF16)),
        [at(width), full((size, width))],
        flops=2 * size * width * width,
        alias={len(ins) + j: j for j in range(len(before))},
    )


def feed(second, grads, ups, downs, biases, before, place, places, grads_place, kind, marks=()):
    size, width = second.shape
    n, units = len(ups), ups[0].shape[1]
    root = 0.5**0.5
    density = (2.0 * jnp.pi) ** -0.5

    def body(*refs):
        second_ref, grads_ref = refs[:2]
        up_refs, down_refs, bias_refs = (refs[2 + j * n : 2 + (j + 1) * n] for j in range(3))
        out_ref, back_ref, d_bias_ref, hidden_ref, inner_ref, rows_ref, grad_rows_ref = refs[
            2 + 3 * n + len(before) + len(marks) :
        ]
        rows_ref[...] = second_ref[...]
        grad_rows_ref[...] = grads_ref[...]
        out = back = 0.0
        for j in range(n):
            cols = slice(j * units, (j + 1) * units)
            u = dot(second_ref[...], up_refs[j][...]) + bias_refs[j][...]
            gh = dot(grads_ref[...], down_refs[j][...], NT)
            below = 0.5 + 0.5 * lax.erf(u * root)
            hidden = (u * below).astype(BF16)
            slope = below + u * (jnp.exp(-0.5 * u * u) * density)
            gi = (gh * slope).astype(BF16)
            hidden_ref[:, cols] = hidden
            inner_ref[:, cols] = gi
            d_bias_ref[:, cols] = jnp.sum(gi.astype(F32), axis=0, keepdims=True)
            out += dot(hidden, down_refs[j][...])
            back += dot(gi, up_refs[j][...], NT)
        out_ref[...] = out.astype(kind)
        back_ref[...] = back.astype(kind)

    ins = (second, grads, *ups, *downs, *biases)
    specs = [full(a.shape) for a in ins]
    specs[1] = pl.BlockSpec((size, width), lambda i: (grads_place, 0))
    at = lambda wide: pl.BlockSpec((size, wide), lambda i: (place, 0))
    outs = (
        shape_of((size, width), kind),
        shape_of((size, width), kind),
        shape_of((1, n * units), F32),
        shape_of((places * size, n * units), BF16),
        shape_of((places * size, n * units), BF16),
        shape_of((places * size, width), BF16),
        shape_of((places * size, width), BF16),
    )
    return call(
        body,
        (1,),
        (),
        ins + tuple(before) + tuple(marks),
        specs + [pl.BlockSpec(memory_space=pl.ANY)] * (len(before) + len(marks)),
        outs,
        [full(o.shape) for o in outs[:3]] + [at(n * units)] * 2 + [at(width)] * 2,
        flops=8 * size * width * n * units,
        alias={len(ins) + j: 3 + j for j in range(len(before))},
        limit=32,
    )


def feed_weights(hidden, inner, second, grads, j, width, pieces):
    total = second.shape[0]
    wide = second.shape[1]
    size = width // pieces

    def body(hidden_ref, inner_ref, second_ref, grads_ref, out_ref):
        up = dot(second_ref[...], inner_ref[...], TN).astype(BF16)
        for p in range(pieces):
            out_ref[2 * p * size : (2 * p + 1) * size, :] = up[p * size : (p + 1) * size]
        down = dot(hidden_ref[...], grads_ref[...], TN).astype(BF16)
        for p in range(pieces):
            out_ref[(2 * p + 1) * size : (2 * p + 2) * size, :] = down[p * size : (p + 1) * size]

    at = pl.BlockSpec((total, width), lambda i: (0, j))
    return call(
        body,
        (1,),
        (),
        (hidden, inner, second, grads),
        [at, at, full(second.shape), full(grads.shape)],
        (shape_of((2 * width, wide), BF16),),
        [full((2 * width, wide))],
        flops=4 * total * width * wide,
        limit=32,
    )[0]


def middle_back(middle, back, back_far, grads, gain, before, h):
    total, width = middle.shape
    size = total // 2

    def body(middle_ref, back_ref, far_ref, grads_ref, gain_ref, *refs):
        grad_ref, round_ref, d_gain_ref, d_shift_ref, d_bias_ref = refs[len(before) :]
        back = back_ref[...] + far_ref[...].astype(F32)
        normal, inverse = standard(middle_ref[...])
        grad = grads_ref[...].astype(F32) + norm_back(normal, inverse, gain_ref[...], back)
        grad_ref[...] = grad
        round_ref[...] = grad.astype(BF16)
        for ref, value in ((d_gain_ref, back * normal), (d_shift_ref, back), (d_bias_ref, grad)):
            ref[...] = jnp.sum(value, axis=0, keepdims=True)

    at = pl.BlockSpec((size, width), lambda i: (h, 0))
    one = shape_of((1, width), F32)
    return call(
        body,
        (1,),
        (),
        (middle, back, back_far, grads, gain, *before),
        [at, full((size, width)), full((size, width)), at, full((1, width))]
        + [pl.BlockSpec(memory_space=pl.ANY)] * len(before),
        (shape_of((total, width), F32), shape_of((total, width), BF16), one, one, one),
        [at, at] + [full((1, width))] * 3,
        flops=10 * total * width,
        alias={5 + j: j for j in range(len(before))},
    )


def attend_back(counts, grad, weights, qkv, attended, first, padded, group):
    total, width = grad.shape
    inner, part = qkv.shape[1], attended.shape[1]
    share = total // padded
    steps, size = share // group, group * padded
    cut = 2 * part

    def body(count_ref, grad_ref, first_ref, w_ref, qkv_ref, att_ref, three_ref, one_ref, two_ref, bias_ref):
        step = pl.program_id(0)
        masks = heads_of(part)
        base = pl.multiple_of(step * size, size)
        for i in range(group):
            where = pl.ds(base + i * padded, padded)
            here = slice(i * padded, (i + 1) * padded)
            count = count_ref[step * group + i]
            ga = dot(grad_ref[where, :], w_ref[inner : inner + part, :], NT).astype(BF16)
            q, k, v = (qkv_ref[here, j * part : (j + 1) * part] for j in range(3))
            exact = probabilities(q, k, count, masks)
            ga_all = stacked(ga, masks)
            gp = dot(ga_all, v, NT)
            gs = exact * (gp - jnp.sum(exact * gp, axis=-1, keepdims=True))
            gs = gs.astype(BF16)
            gq = merged(dot(gs, k), masks, padded) * HD**-0.5
            gk = dot(gs, stacked(q, masks), TN) * HD**-0.5
            gv = dot(exact.astype(BF16), ga_all, TN)
            three_ref[where, :] = jnp.concatenate([x.astype(BF16) for x in (gq, gk, gv)], axis=1)

        @pl.when(step == steps - 1)
        def _():
            one_ref[...] = dot(three_ref[:, :cut], first_ref[...], TN).astype(BF16)
            two_ref[: inner - cut, :] = dot(three_ref[:, cut:], first_ref[...], TN).astype(BF16)
            two_ref[inner - cut :, :] = dot(att_ref[...], grad_ref[...], TN).astype(BF16)
            bias_ref[...] = jnp.sum(three_ref[...].astype(F32), axis=0, keepdims=True)

    ins = (grad, first, weights, qkv, attended)
    specs = [full(a.shape) for a in ins]
    specs[3] = rows(size, inner)
    outs = (
        shape_of((total, inner), BF16),
        shape_of((cut, width), BF16),
        shape_of((inner - cut + part, width), BF16),
        shape_of((1, inner), F32),
    )
    return call(
        body,
        (steps,),
        (counts,),
        ins,
        specs,
        outs,
        [full(o.shape) for o in outs],
        flops=5 * total * width * width,
        limit=56,
    )


def close(counts, middle, outs, outs_far, b_fc2, padded, slots):
    total, width = middle.shape
    share = total // padded
    half = share // 2

    def body(count_ref, middle_ref, *refs):
        out_refs, far_refs, bias_ref, layer_ref = refs[:2], refs[2:4], refs[4], refs[5]
        for i in range(share):
            h, here = i // half, slice(i % half * padded, (i % half + 1) * padded)
            layer = middle_ref[i * padded : (i + 1) * padded, :] + bias_ref[...]
            layer = layer + (out_refs[h][here, :] + far_refs[h][here, :].astype(F32))
            seen = lax.broadcasted_iota(jnp.int32, (padded, 1), 0) < count_ref[i]
            layer_ref[i] = jnp.where(seen, layer, 0.0).astype(BF16)[0:slots]

    ins = (middle, *outs, *outs_far, b_fc2)
    shape = (share, slots, width)
    return call(
        body,
        (1,),
        (counts,),
        ins,
        [full(a.shape) for a in ins],
        (shape_of(shape, BF16),),
        [full(shape)],
        flops=4 * total * width,
    )[0]


def finish(keep, tokens, threes, weights, grad, gain, marks, patch_count, padded):
    total, width = tokens.shape
    share, n, inner = total // padded, len(threes), threes[0].shape[1]

    def body(keep_ref, tokens_ref, grad_ref, gain_ref, *refs):
        three_refs, w_refs = refs[:n], refs[n : 2 * n]
        out_ref, d_gain_ref, d_shift_ref = refs[2 * n + len(marks) :]
        back = sum(dot(t[...], w[:inner, :]) for t, w in zip(three_refs, w_refs))
        normal, inverse = standard(tokens_ref[...].astype(F32))
        grad = grad_ref[...] + norm_back(normal, inverse, gain_ref[...], back)
        add_row(d_gain_ref, back * normal)
        add_row(d_shift_ref, back)
        image = pl.program_id(0)
        picks = slots_matrix(keep_ref[pl.ds(image, 1), :], patch_count)
        high = grad.astype(BF16)
        low = (grad - high.astype(F32)).astype(BF16)
        out_ref[0] = dot(picks, high) + dot(picks, low)

    one = shape_of((1, width), F32)
    return call(
        body,
        (share,),
        (),
        (keep, tokens, grad, gain, *threes, *weights, *marks),
        [full(keep.shape), rows(padded, width), rows(padded, width), full((1, width))]
        + [rows(padded, inner)] * n
        + [full(w.shape) for w in weights]
        + [pl.BlockSpec(memory_space=pl.ANY)] * len(marks),
        (shape_of((share, patch_count, width), F32), one, one),
        [pl.BlockSpec((1, patch_count, width), lambda i, *_: (i, 0, 0))] + [full((1, width))] * 2,
        flops=2 * total * (n * inner + 2 * patch_count) * width,
        limit=56,
    )


def swap(value, axis, bit):
    size = lax.axis_size(axis)
    return lax.ppermute(value, axis, [(i, i ^ bit) for i in range(size)])


def after(value, *others):
    return lax.optimization_barrier((value, *others))[0]


def rows_at(value, start, size):
    return lax.dynamic_slice_in_dim(value, start, size, 0)


def whole(mine, other, bit):
    return jnp.where(
        bit == 0, jnp.concatenate([mine, other], axis=0), jnp.concatenate([other, mine], axis=0)
    )


def place_bit(bit):
    return (lax.axis_index("dp") // bit) % 2


def added(terms, start, size):
    return sum(rows_at(value, offset + start, size).astype(F32) for value, offset in terms)


def deal(value, stride):
    size = lax.axis_size("dp")
    groups = [list(range(first, size, stride)) for first in range(stride)]
    return lax.all_to_all(
        value, "dp", split_axis=0, concat_axis=0, axis_index_groups=groups, tiled=True
    )


def split_high(value):
    high = lax.reduce_precision(value, 8, 7)
    return jnp.concatenate([high.astype(BF16), (value - high).astype(BF16)], axis=0)


def split_exact(value):
    parts = []
    for _ in range(3):
        part = lax.reduce_precision(value, 8, 7)
        parts.append(part.astype(BF16))
        value = value - part
    return jnp.concatenate(parts, axis=0)


class Chain:
    def __init__(self, near, far, route):
        self.near, self.far = [(n, 0) for n in near], [(f, 0) for f in far]
        self.rows = near[0].shape[0]
        self.route = route
        self.value = None
        self.ride = None

    def send(self, *others):
        kind, bit = self.route[0]
        last = self.value if self.value is not None else self.near[-1][0]
        if others:
            last = after(last, *others)
            if self.value is not None:
                self.value = last
            else:
                self.near[-1] = (last, self.near[-1][1])
        if kind == "far":
            out = added(self.far, 0, self.rows).astype(BF16)
            self.sent = swap(out, "tensor", 2)
        elif kind == "sum":
            self.rows //= 2
            self.mine = place_bit(bit)
            start = (1 - self.mine) * self.rows
            parts = [added(self.near, start, self.rows).astype(BF16)]
            if self.far:
                parts.append(added(self.far, start, self.rows).astype(BF16))
            out = jnp.concatenate(parts, axis=0) if len(parts) > 1 else parts[0]
            self.sent = swap(out, "dp", bit)
        elif kind == "part":
            out = added(self.near, 0, self.rows).astype(BF16)
            self.sent = deal(out, bit)
            self.rows //= lax.axis_size("dp") // bit
        elif kind == "gather":
            if self.value is None:
                self.value = added(self.near, 0, self.rows).astype(BF16)
            out = jnp.broadcast_to(self.value[None], (lax.axis_size("dp") // bit, *self.value.shape))
            out = out.reshape(-1, self.value.shape[1])
            self.sent = deal(out, bit)
        else:
            if self.value is None:
                self.value = added(self.near, 0, self.rows).astype(BF16)
            out = self.value
            if self.ride is not None:
                self.ride = split_high(self.ride)
                out = jnp.concatenate([out, self.ride], axis=0)
            self.sent = swap(out, "dp", bit)
        self.out = out
        return out

    def receive(self):
        kind, bit = self.route.pop(0)
        if kind == "far":
            self.near.append((self.sent, 0))
            self.far = []
        elif kind == "sum":
            shift = self.mine * self.rows
            self.near = [(value, offset + shift) for value, offset in self.near] + [(self.sent, 0)]
            if self.far:
                self.far = [(value, offset + shift) for value, offset in self.far]
                self.far.append((self.sent, self.rows))
        elif kind == "part":
            self.near = [(self.sent, j) for j in range(0, self.sent.shape[0], self.rows)]
        elif kind == "gather":
            self.value = self.sent
        else:
            size = self.value.shape[0]
            if self.ride is not None:
                count = self.ride.shape[0] // 2
                other = self.sent[size:]
                self.ride = sum(
                    part[:count].astype(F32) + part[count:].astype(F32) for part in (self.ride, other)
                )
            self.value = whole(self.value, self.sent[:size], place_bit(bit))

    def step(self, *others):
        self.receive()
        if self.route:
            return self.send(*others)
        if others:
            self.value = after(self.value, *others)
        return self.value


def routes():
    bits, size = [], lax.axis_size("dp")
    while 2 ** len(bits) < size:
        bits.append(2 ** len(bits))
    turned = bits[1:] + bits[:1]
    sums = lambda order: [("sum", bit) for bit in order]
    joins = lambda order: [("join", bit) for bit in reversed(order)]
    return sums(bits) + joins(bits), sums(turned) + joins(turned)


def shards(
    patches,
    keep_slots,
    visible_count,
    gain_one,
    shift_one,
    w_qkv,
    b_qv,
    w_out,
    b_out,
    gain_two,
    shift_two,
    w_fc1,
    b_fc1,
    w_fc2,
    b_fc2,
    out_grad,
):
    images, slots = keep_slots.shape
    patch_count, width = patches.shape[1:]
    tensor = lax.axis_size("tensor")
    spot = lax.axis_index("tensor")
    share = images // tensor
    padded = -(-slots // 8) * 8
    part, units = w_qkv.shape[2], w_fc1.shape[1]
    inner = 3 * part
    origin = spot * share
    counts = lax.dynamic_slice_in_dim(visible_count, origin, share, 0)
    keep = lax.dynamic_slice_in_dim(keep_slots, origin, share, 0)
    keep = jnp.pad(keep, ((0, 0), (0, padded - slots)), constant_values=-1)
    patches = lax.dynamic_slice_in_dim(patches, origin, share, 0)
    line = lambda vector: vector.reshape(1, -1)

    bias = jnp.concatenate([b_qv[0], jnp.zeros_like(b_qv[0]), b_qv[1], jnp.zeros_like(b_qv[0])])
    bias = split_exact(line(bias))
    bias = jnp.pad(bias, ((0, 16 - bias.shape[0]), (0, 0)))
    mix = jnp.concatenate([w_qkv.transpose(0, 2, 1).reshape(inner, width), w_out, bias], axis=0)
    far_mix, near_mix = swap(mix, "tensor", 2), swap(mix, "tensor", 1)
    units_biases = [line(b_fc1), swap(line(b_fc1), "tensor", 1)]

    tokens, first, *both = begin(
        counts,
        keep,
        patches,
        out_grad,
        line(gain_one),
        line(shift_one),
        (mix, near_mix),
        inner,
    )
    grad_rows, g_b_fc2, both = both[0], both[1], both[2:]
    three, attended = both[:2], both[2:]
    far_grads = swap(grad_rows, "tensor", 2)
    cross_mix = swap(after(far_mix, first), "tensor", 1)
    mixes = [mix, near_mix, far_mix, cross_mix]
    for r in (2, 3):
        qkv, mixed = attend(counts, after(first, attended[-1]), mixes[r : r + 1], padded, inner)
        three, attended = three + [qkv], attended + [mixed]
    before, seconds = (), []
    for h in range(2):
        middle, second = join(
            tokens,
            attended,
            mixes,
            line(b_out),
            line(gain_two),
            line(shift_two),
            before,
            h,
        )
        before = (middle,)
        seconds.append(second)
    far_seconds = [swap(seconds[0], "tensor", 2)]
    far_seconds.append(swap(seconds[1], "tensor", 2))
    near_up, near_down = (swap(w, "tensor", 1) for w in (w_fc1, w_fc2))
    g_b_fc1, own, far, before = 0.0, [], [], ()

    def feeding(place, second, grads, kind, *others, marks=()):
        nonlocal g_b_fc1, before
        out, back, d_bias, *before = feed(
            after(second, *others),
            grads,
            (w_fc1, near_up),
            (w_fc2, near_down),
            units_biases,
            before,
            place,
            4,
            place % 2,
            kind,
            marks,
        )
        g_b_fc1 += d_bias
        return out, back

    own.append(feeding(0, seconds[0], grad_rows, F32, seconds[1]))
    own.append(feeding(1, seconds[1], grad_rows, F32))
    far.append(feeding(2, after(far_seconds[0], own[1][0]), far_grads, BF16))
    backs = [swap(far[0][1], "tensor", 2)]
    mark = swap(far_seconds[0][:8, :128], "tensor", 1)
    far.append(feeding(3, after(far_seconds[1], far[0][0]), far_grads, BF16, marks=(mark,)))
    backs.append(swap(far[1][1], "tensor", 2))
    pieces = lax.axis_size("dp")
    units_one = feed_weights(*before, 1, units, pieces)
    near = swap(units_one, "tensor", 1)
    hidden, *rest = before
    units_zero = feed_weights(after(hidden, units_one), *rest, 0, units, pieces)
    first_route, second_route = routes()
    parts, before = [], ()
    for h in range(2):
        back = after(backs[h], units_zero, *before)
        *before, d_gain, d_shift, d_bias = middle_back(
            middle, own[h][1], back, grad_rows, line(gain_two), before, h
        )
        parts.append((d_gain, d_shift, d_bias))
    g_gain_two, g_shift_two, g_b_out = (a + b for a, b in zip(*parts))
    grad_middle, grad_round = before
    both = Chain([units_zero, near], [], [("sum", 1), ("part", 2), ("gather", 2), ("join", 1)])
    sent = [both.send(units_zero)]
    mlp = [swap(after(far[h][0], *sent), "tensor", 2) for h in range(2)]

    backward = [None] * 4
    g_b_qkv = [None] * 4

    def attending_back(r, *others):
        backward[r], one, two, g_b_qkv[r] = attend_back(
            counts, after(grad_round, *others), mixes[r], three[r], attended[r], first, padded, 2
        )
        return one, two

    one, two = attending_back(3, *sent)
    far = [swap(one, "tensor", 1), swap(two, "tensor", 1)]
    one, two = attending_back(2)
    far = jnp.concatenate(
        [
            (a.astype(F32) + after(b, two).astype(F32)).astype(BF16)
            for a, b in ((one, far[0]), (two, far[1]))
        ]
    )
    sent = [both.step(two), far]
    far = swap(far, "tensor", 2)
    one, two = attending_back(1, *sent)
    near = [swap(one, "tensor", 1), swap(two, "tensor", 1)]
    one, two = attending_back(0, *mlp)
    ones = Chain([one, near[0], far], [], list(first_route))
    twos = Chain([two, near[1]], [], list(second_route))
    twos.near.append((far, one.shape[0]))
    sent = [ones.send(two), twos.send(two), both.step(two)]
    marks = (swap(both.out[:8, :128], "tensor", 1),)
    grad_patches, g_gain_one, g_shift_one = finish(
        keep,
        after(tokens, *sent),
        backward,
        mixes,
        grad_middle,
        line(gain_one),
        marks,
        patch_count,
        padded,
    )
    shared = jnp.concatenate([g_gain_one, g_shift_one, g_b_out, g_gain_two, g_shift_two, g_b_fc2])
    zero = jnp.zeros((1, units), F32)
    g_b_fc1 = [g_b_fc1[:, :units], g_b_fc1[:, units:], zero, zero]
    local = jnp.concatenate([jnp.concatenate(g_b_qkv), jnp.concatenate(g_b_fc1)], axis=1)
    size = -(-local.shape[1] // width)
    local = jnp.pad(local, ((0, 0), (0, size * width - local.shape[1])))
    local = local.reshape(tensor * size, width)
    small = jnp.concatenate([shared, local], axis=0)
    other = swap(small, "tensor", 1)
    halves = lambda a, b: (a[:6] + b[:6], a[6:].reshape(tensor, size, width), b[6:].reshape(tensor, size, width))
    shared, mine, theirs = halves(small, other)
    pairs = jnp.stack([mine[0] + theirs[1], mine[2] + theirs[3]])
    small = jnp.concatenate([shared, pairs.reshape(2 * size, width)], axis=0)
    other = swap(small, "tensor", 2)
    ride = jnp.concatenate([small[:6] + other[:6], small[6 : 6 + size] + other[6 + size :]], axis=0)
    last = g_shift_one
    while ones.route[1][0] == "sum":
        last = ones.step(last)
        last = twos.step(last)
    last = both.step(last)
    layer_out = close(
        counts,
        middle,
        [o[0] for o in own],
        [after(m, last) for m in mlp],
        line(b_fc2),
        padded,
        slots,
    )
    twos.ride = ride
    while ones.route:
        last = ones.step(last)
        last = twos.step(last)
    last = both.step(last)
    ride = twos.ride
    both = both.value.reshape(pieces, 2, units // pieces, width).astype(F32)
    grad_w_fc1, grad_w_fc2 = (both[:, j].reshape(units, width) for j in range(2))
    qk, vo = ones.value.astype(F32), twos.value.astype(F32)
    local = ride[6:].reshape(1, -1)[0]
    shared = ride[:6]
    grad_w_qkv = jnp.concatenate([qk, vo[:part]], axis=0).reshape(3, part, width).transpose(0, 2, 1)
    grad_b_qv = jnp.stack([local[:part], local[2 * part : inner]])
    return (
        layer_out,
        grad_patches,
        shared[0],
        shared[1],
        grad_w_qkv,
        grad_b_qv,
        vo[part:],
        shared[2],
        shared[3],
        shared[4],
        grad_w_fc1,
        local[inner : inner + units],
        grad_w_fc2,
        shared[5],
    )


def solution(mesh):
    return jax.shard_map(
        shards,
        mesh=mesh,
        in_specs=(
            P("dp", None, None),
            P("dp", None),
            P("dp"),
            P(),
            P(),
            P(None, None, "tensor"),
            P(None, "tensor"),
            P("tensor", None),
            P(),
            P(),
            P(),
            P(None, "tensor"),
            P("tensor"),
            P("tensor", None),
            P(),
            P(("dp", "tensor"), None, None),
        ),
        out_specs=(
            P(("dp", "tensor"), None, None),
            P(("dp", "tensor"), None, None),
            P(),
            P(),
            P(None, None, "tensor"),
            P(None, "tensor"),
            P("tensor", None),
            P(),
            P(),
            P(),
            P(None, "tensor"),
            P("tensor"),
            P("tensor", None),
            P(),
        ),
        check_vma=False,
    )
```

```python
import functools

import jax
import jax.numpy as jnp
from jax import lax
from jax.experimental import pallas as pl
from jax.experimental.pallas import tpu as pltpu
from jax.sharding import PartitionSpec as P

HD = 64
EPSILON = 1e-06
MASKED = -1000000000.0
F32 = jnp.float32
BF16 = jnp.bfloat16
VMEM = pltpu.VMEM
NN = (((1,), (0,)), ((), ()))
NT = (((1,), (1,)), ((), ()))
TN = (((0,), (0,)), ((), ()))


def dot(left, right, dims=NN):
    return lax.dot_general(left, right, dims, preferred_element_type=F32)


def standard(inputs):
    average = jnp.mean(inputs, axis=-1, keepdims=True)
    centered = inputs - average
    spread = jnp.mean(centered * centered, axis=-1, keepdims=True)
    inverse = lax.rsqrt(spread + EPSILON)
    return centered * inverse, inverse


def norm_back(normal, inverse, gain, gradient):
    scaled = gradient * gain
    first = jnp.mean(scaled, axis=-1, keepdims=True)
    second = jnp.mean(scaled * normal, axis=-1, keepdims=True)
    return inverse * (scaled - first - normal * second)


def slots_matrix(keep_row, patch_count):
    places = lax.broadcasted_iota(jnp.int32, (patch_count, keep_row.shape[1]), 0)
    return (places == keep_row).astype(F32).astype(BF16)


def add_row(ref, value):
    row = jnp.sum(value, axis=0, keepdims=True)

    @pl.when(pl.program_id(0) == 0)
    def _():
        ref[...] = jnp.zeros_like(ref)

    ref[...] += row


def full(shape):
    return pl.BlockSpec(shape, lambda i, *_: (0,) * len(shape))


def rows(count, width):
    return pl.BlockSpec((count, width), lambda i, *_: (i, 0))


def call(body, grid, scalars, ins, in_specs, outs, out_specs, scratch=(), flops=0, alias=None, limit=24):
    size = sum(a.size * a.dtype.itemsize for a in ins)
    size += sum(o.size * o.dtype.itemsize for o in outs)
    return pl.pallas_call(
        body,
        out_shape=outs,
        grid_spec=pltpu.PrefetchScalarGridSpec(
            num_scalar_prefetch=len(scalars),
            grid=grid,
            in_specs=in_specs,
            out_specs=out_specs,
            scratch_shapes=scratch,
        ),
        compiler_params=pltpu.CompilerParams(vmem_limit_bytes=limit * 2**20),
        input_output_aliases=alias or {},
        cost_estimate=pl.CostEstimate(flops=100 * flops, bytes_accessed=100 * size, transcendentals=0),
    )(*scalars, *ins)


def shape_of(shape, kind):
    return jax.ShapeDtypeStruct(shape, kind)


def heads_of(width):
    lanes = lax.broadcasted_iota(jnp.int32, (1, width), 1) // HD
    return [(lanes == h).astype(BF16) for h in range(width // HD)]


def stacked(values, masks):
    return jnp.concatenate([values * m for m in masks], axis=0)


def merged(values, masks, length):
    lanes = lax.broadcasted_iota(jnp.int32, (1, values.shape[1]), 1) // HD
    result = values[0:length]
    for h in range(1, len(masks)):
        result = jnp.where(lanes == h, values[h * length : (h + 1) * length], result)
    return result


def probabilities(queries, keys, count, masks):
    scores = dot(stacked(queries, masks), keys, NT) * HD**-0.5
    seen = lax.broadcasted_iota(jnp.int32, (1, keys.shape[0]), 1) < count
    scores = jnp.where(seen, scores, MASKED)
    powers = jnp.exp(scores - jnp.max(scores, axis=-1, keepdims=True))
    return powers / jnp.sum(powers, axis=-1, keepdims=True)


def attention(first, w_ref, counts, masks, qkv_ref, out_ref, padded):
    inner = qkv_ref.shape[1]
    part = inner // 3
    bias = jnp.sum(w_ref[inner + part :, :].astype(F32), axis=0, keepdims=True)[:, :inner]
    qkv = (dot(first, w_ref[:inner, :], NT) + bias).astype(BF16)
    qkv_ref[...] = qkv
    for g, count in enumerate(counts):
        here = slice(g * padded, (g + 1) * padded)
        q, k, v = (qkv[here, j * part : (j + 1) * part] for j in range(3))
        chances = probabilities(q, k, count, masks).astype(BF16)
        out_ref[here, :] = merged(dot(chances, v), masks, padded).astype(BF16)


def begin(counts, keep, patches, out_grad, gain, shift, weights, inner):
    share, padded = keep.shape
    slots = out_grad.shape[1]
    patch_count, width = patches.shape[1:]
    total, n = share * padded, len(weights)
    part = inner // 3
    group = 2
    size = group * padded

    def body(count_ref, keep_ref, patch_ref, grad_ref, gain_ref, shift_ref, *refs):
        w_refs, outs = refs[:n], refs[n:]
        tokens_ref, first_ref, rows_ref, sum_ref = outs[:4]
        qkv_refs, att_refs = outs[4 : 4 + n], outs[4 + n :]
        masks = heads_of(part)
        total_sum = jnp.zeros((1, width), F32)
        for g in range(group):
            image = pl.program_id(0) * group + g
            here = slice(g * padded, (g + 1) * padded)
            picks = slots_matrix(keep_ref[pl.ds(image, 1), :], patch_count)
            tokens = dot(picks, patch_ref[g], TN)
            tokens_ref[here, :] = tokens.astype(BF16)
            normal, _ = standard(tokens)
            first = (normal * gain_ref[...] + shift_ref[...]).astype(BF16)
            first_ref[here, :] = first
            seen = lax.broadcasted_iota(jnp.int32, (slots, 1), 0) < count_ref[image]
            grads = jnp.where(seen, grad_ref[g].astype(F32), 0.0)
            rows_ref[here, :] = jnp.zeros((padded, width), BF16)
            rows_ref[g * padded : g * padded + slots, :] = grads.astype(BF16)
            total_sum += jnp.sum(grads, axis=0, keepdims=True)
        counts = [count_ref[pl.program_id(0) * group + g] for g in range(group)]
        for w_ref, qkv_ref, att_ref in zip(w_refs, qkv_refs, att_refs):
            attention(first_ref[...], w_ref, counts, masks, qkv_ref, att_ref, padded)
        add_row(sum_ref, total_sum)

    return call(
        body,
        (share // group,),
        (counts,),
        (keep, patches, out_grad, gain, shift, *weights),
        [
            full(keep.shape),
            pl.BlockSpec((group, patch_count, width), lambda i, *_: (i, 0, 0)),
            pl.BlockSpec((group, slots, width), lambda i, *_: (i, 0, 0)),
            full(gain.shape),
            full(shift.shape),
        ]
        + [full(w.shape) for w in weights],
        (shape_of((total, width), BF16),) * 3
        + (shape_of((1, width), F32),)
        + (shape_of((total, inner), BF16),) * n
        + (shape_of((total, part), BF16),) * n,
        [rows(size, width)] * 3
        + [full((1, width))]
        + [rows(size, inner)] * n
        + [rows(size, part)] * n,
        flops=2 * total * (patch_count + n * inner) * width,
    )


def attend(counts, first, weights, padded, inner):
    total, width = first.shape
    n, part = len(weights), inner // 3
    group = 2
    size = group * padded

    def body(count_ref, first_ref, *refs):
        w_refs, qkv_refs, att_refs = refs[:n], refs[n : 2 * n], refs[2 * n :]
        masks = heads_of(part)
        counts = [count_ref[pl.program_id(0) * group + g] for g in range(group)]
        for w_ref, qkv_ref, att_ref in zip(w_refs, qkv_refs, att_refs):
            attention(first_ref[...], w_ref, counts, masks, qkv_ref, att_ref, padded)

    return call(
        body,
        (total // size,),
        (counts,),
        (first, *weights),
        [rows(size, width)] + [full(w.shape) for w in weights],
        (shape_of((total, inner), BF16),) * n + (shape_of((total, part), BF16),) * n,
        [rows(size, inner)] * n + [rows(size, part)] * n,
        flops=2 * total * n * inner * width,
    )


def join(tokens, attended, w_outs, b_out, gain, shift, before, h):
    total, width = tokens.shape
    size, n = total // 2, len(attended)
    part = attended[0].shape[1]

    def body(tokens_ref, *refs):
        att_refs, o_refs, refs = refs[:n], refs[n : 2 * n], refs[2 * n :]
        bias_ref, gain_ref, shift_ref = refs[:3]
        middle_ref, second_ref = refs[3 + len(before) :]
        rows_of_out = slice(3 * part, 4 * part)
        branch = sum(dot(a[...], o[rows_of_out, :]) for a, o in zip(att_refs, o_refs))
        middle = tokens_ref[...].astype(F32) + branch + bias_ref[...]
        middle_ref[...] = middle
        normal, _ = standard(middle)
        second_ref[...] = (normal * gain_ref[...] + shift_ref[...]).astype(BF16)

    at = lambda wide: pl.BlockSpec((size, wide), lambda i: (h, 0))
    ins = (tokens, *attended, *w_outs, b_out, gain, shift)
    specs = [at(width)] + [at(part)] * n + [full(w.shape) for w in ins[1 + n :]]
    return call(
        body,
        (1,),
        (),
        ins + tuple(before),
        specs + [pl.BlockSpec(memory_space=pl.ANY)] * len(before),
        (shape_of((total, width), F32), shape_of((size, width), BF16)),
        [at(width), full((size, width))],
        flops=2 * size * width * width,
        alias={len(ins) + j: j for j in range(len(before))},
    )


def unwritten(shapes, first):
    def body(first_ref, *refs):
        refs[-1][...] = jnp.zeros_like(refs[-1])

    outs = (*(shape_of(shape, BF16) for shape in shapes), shape_of((8, 128), BF16))
    return pl.pallas_call(
        body,
        out_shape=outs,
        in_specs=[pl.BlockSpec(memory_space=pl.ANY)],
        out_specs=[pl.BlockSpec(memory_space=pl.ANY)] * len(shapes) + [pl.BlockSpec(memory_space=pltpu.VMEM)],
        compiler_params=pltpu.CompilerParams(vmem_limit_bytes=2**20),
    )(first)


def feed(second, grads, ups, downs, biases, before, place, mark):
    size, width = second.shape
    n, units = len(ups), ups[0].shape[1]
    root = 0.5**0.5
    density = (2.0 * jnp.pi) ** -0.5

    def body(place_ref, *refs):
        second_ref, grads_ref = refs[:2]
        up_refs, down_refs, bias_refs = (refs[2 + j * n : 2 + (j + 1) * n] for j in range(3))
        out_ref, back_ref, d_bias_ref, hidden_ref, inner_ref, rows_ref, grad_rows_ref = refs[
            2 + 3 * n + len(before) + 1 :
        ]
        rows_ref[...] = second_ref[...]
        grad_rows_ref[...] = grads_ref[...]
        out = back = 0.0
        for j in range(n):
            cols = slice(j * units, (j + 1) * units)
            u = dot(second_ref[...], up_refs[j][...]) + bias_refs[j][...]
            gh = dot(grads_ref[...], down_refs[j][...], NT)
            below = 0.5 + 0.5 * lax.erf(u * root)
            hidden = (u * below).astype(BF16)
            slope = below + u * (jnp.exp(-0.5 * u * u) * density)
            gi = (gh * slope).astype(BF16)
            hidden_ref[:, cols] = hidden
            inner_ref[:, cols] = gi
            d_bias_ref[:, cols] = jnp.sum(gi.astype(F32), axis=0, keepdims=True)
            out += dot(hidden, down_refs[j][...])
            back += dot(gi, up_refs[j][...], NT)
        out_ref[...] = out.astype(BF16)
        back_ref[...] = back.astype(BF16)

    ins = (second, grads, *ups, *downs, *biases)
    specs = [full(a.shape) for a in ins]
    specs[1] = pl.BlockSpec((size, width), lambda i, p: (p[0] % 2, 0))
    at = lambda wide: pl.BlockSpec((size, wide), lambda i, p: (p[0], 0))
    outs = (
        shape_of((size, width), BF16),
        shape_of((size, width), BF16),
        shape_of((1, n * units), F32),
        *(shape_of(a.shape, a.dtype) for a in before),
    )
    return call(
        body,
        (1,),
        (place,),
        ins + tuple(before) + (mark,),
        specs + [pl.BlockSpec(memory_space=pl.ANY)] * (len(before) + 1),
        outs,
        [full(o.shape) for o in outs[:3]] + [at(n * units)] * 2 + [at(width)] * 2,
        flops=8 * size * width * n * units,
        alias={1 + len(ins) + j: 3 + j for j in range(len(before))},
        limit=32,
    )


def feed_weights(hidden, inner, second, grads, j, width, pieces):
    total = second.shape[0]
    wide = second.shape[1]
    size = width // pieces

    def body(place_ref, hidden_ref, inner_ref, second_ref, grads_ref, out_ref):
        up = dot(second_ref[...], inner_ref[...], TN).astype(BF16)
        for p in range(pieces):
            out_ref[2 * p * size : (2 * p + 1) * size, :] = up[p * size : (p + 1) * size]
        down = dot(hidden_ref[...], grads_ref[...], TN).astype(BF16)
        for p in range(pieces):
            out_ref[(2 * p + 1) * size : (2 * p + 2) * size, :] = down[p * size : (p + 1) * size]

    at = pl.BlockSpec((total, width), lambda i, p: (0, p[0]))
    return call(
        body,
        (1,),
        (j,),
        (hidden, inner, second, grads),
        [at, at, full(second.shape), full(grads.shape)],
        (shape_of((2 * width, wide), BF16),),
        [full((2 * width, wide))],
        flops=4 * total * width * wide,
        limit=32,
    )[0]


def middle_back(middle, back, back_far, grads, gain, before, h):
    total, width = middle.shape
    size = total // 2

    def body(middle_ref, back_ref, far_ref, grads_ref, gain_ref, *refs):
        grad_ref, round_ref, d_gain_ref, d_shift_ref, d_bias_ref = refs[len(before) :]
        back = back_ref[...].astype(F32) + far_ref[...].astype(F32)
        normal, inverse = standard(middle_ref[...])
        grad = grads_ref[...].astype(F32) + norm_back(normal, inverse, gain_ref[...], back)
        grad_ref[...] = grad
        round_ref[...] = grad.astype(BF16)
        for ref, value in ((d_gain_ref, back * normal), (d_shift_ref, back), (d_bias_ref, grad)):
            ref[...] = jnp.sum(value, axis=0, keepdims=True)

    at = pl.BlockSpec((size, width), lambda i: (h, 0))
    one = shape_of((1, width), F32)
    return call(
        body,
        (1,),
        (),
        (middle, back, back_far, grads, gain, *before),
        [at, full((size, width)), full((size, width)), at, full((1, width))]
        + [pl.BlockSpec(memory_space=pl.ANY)] * len(before),
        (shape_of((total, width), F32), shape_of((total, width), BF16), one, one, one),
        [at, at] + [full((1, width))] * 3,
        flops=10 * total * width,
        alias={5 + j: j for j in range(len(before))},
    )


def attend_back(counts, grad, weights, qkv, attended, first, padded, group):
    total, width = grad.shape
    inner, part = qkv.shape[1], attended.shape[1]
    share = total // padded
    steps, size = share // group, group * padded
    cut = 2 * part

    def body(count_ref, grad_ref, first_ref, w_ref, qkv_ref, att_ref, three_ref, one_ref, two_ref, bias_ref):
        step = pl.program_id(0)
        masks = heads_of(part)
        base = pl.multiple_of(step * size, size)
        w_out = w_ref[inner : inner + part, :]
        ga_group = dot(grad_ref[pl.ds(base, size), :], w_out, NT).astype(BF16)
        for i in range(group):
            where = pl.ds(base + i * padded, padded)
            here = slice(i * padded, (i + 1) * padded)
            count = count_ref[step * group + i]
            ga = ga_group[here]
            q, k, v = (qkv_ref[here, j * part : (j + 1) * part] for j in range(3))
            exact = probabilities(q, k, count, masks)
            ga_all = stacked(ga, masks)
            gp = dot(ga_all, v, NT)
            gs = exact * (gp - jnp.sum(exact * gp, axis=-1, keepdims=True))
            gs = gs.astype(BF16)
            gq = merged(dot(gs, k), masks, padded) * HD**-0.5
            gk = dot(gs, stacked(q, masks), TN) * HD**-0.5
            gv = dot(exact.astype(BF16), ga_all, TN)
            three_ref[where, :] = jnp.concatenate([x.astype(BF16) for x in (gq, gk, gv)], axis=1)

        @pl.when(step == steps - 1)
        def _():
            one_ref[...] = dot(three_ref[:, :cut], first_ref[...], TN).astype(BF16)
            two_ref[: inner - cut, :] = dot(three_ref[:, cut:], first_ref[...], TN).astype(BF16)
            two_ref[inner - cut :, :] = dot(att_ref[...], grad_ref[...], TN).astype(BF16)
            bias_ref[...] = jnp.sum(three_ref[...].astype(F32), axis=0, keepdims=True)

    ins = (grad, first, weights, qkv, attended)
    specs = [full(a.shape) for a in ins]
    specs[3] = rows(size, inner)
    outs = (
        shape_of((total, inner), BF16),
        shape_of((cut, width), BF16),
        shape_of((inner - cut + part, width), BF16),
        shape_of((1, inner), F32),
    )
    return call(
        body,
        (steps,),
        (counts,),
        ins,
        specs,
        outs,
        [full(o.shape) for o in outs],
        flops=5 * total * width * width,
        limit=56,
    )


def close(counts, middle, outs, outs_far, b_fc2, padded, slots):
    total, width = middle.shape
    share = total // padded
    half = share // 2

    def body(count_ref, middle_ref, *refs):
        out_refs, far_refs, bias_ref, layer_ref = refs[:2], refs[2:4], refs[4], refs[5]
        for i in range(share):
            h, here = i // half, slice(i % half * padded, (i % half + 1) * padded)
            layer = middle_ref[i * padded : (i + 1) * padded, :] + bias_ref[...]
            layer = layer + (out_refs[h][here, :].astype(F32) + far_refs[h][here, :].astype(F32))
            seen = lax.broadcasted_iota(jnp.int32, (padded, 1), 0) < count_ref[i]
            layer_ref[i] = jnp.where(seen, layer, 0.0).astype(BF16)[0:slots]

    ins = (middle, *outs, *outs_far, b_fc2)
    shape = (share, slots, width)
    return call(
        body,
        (1,),
        (counts,),
        ins,
        [full(a.shape) for a in ins],
        (shape_of(shape, BF16),),
        [full(shape)],
        flops=4 * total * width,
    )[0]


def finish(keep, tokens, threes, weights, grad, gain, marks, patch_count, padded):
    total, width = tokens.shape
    share, n, inner = total // padded, len(threes), threes[0].shape[1]
    group = share // 2
    size = group * padded

    def body(keep_ref, tokens_ref, grad_ref, gain_ref, *refs):
        three_refs, w_refs = refs[:n], refs[n : 2 * n]
        out_ref, d_gain_ref, d_shift_ref = refs[2 * n + len(marks) :]
        back = sum(dot(t[...], w[:inner, :]) for t, w in zip(three_refs, w_refs))
        normal, inverse = standard(tokens_ref[...].astype(F32))
        grad = grad_ref[...] + norm_back(normal, inverse, gain_ref[...], back)
        add_row(d_gain_ref, back * normal)
        add_row(d_shift_ref, back)
        high = grad.astype(BF16)
        low = (grad - high.astype(F32)).astype(BF16)
        for g in range(group):
            here = slice(g * padded, (g + 1) * padded)
            image = pl.program_id(0) * group + g
            picks = slots_matrix(keep_ref[pl.ds(image, 1), :], patch_count)
            out_ref[g] = dot(picks, high[here]) + dot(picks, low[here])

    one = shape_of((1, width), F32)
    return call(
        body,
        (2,),
        (),
        (keep, tokens, grad, gain, *threes, *weights, *marks),
        [full(keep.shape), rows(size, width), rows(size, width), full((1, width))]
        + [rows(size, inner)] * n
        + [full(w.shape) for w in weights]
        + [pl.BlockSpec(memory_space=pl.ANY)] * len(marks),
        (shape_of((share, patch_count, width), F32), one, one),
        [pl.BlockSpec((group, patch_count, width), lambda i, *_: (i, 0, 0))] + [full((1, width))] * 2,
        flops=2 * total * (n * inner + 2 * patch_count) * width,
        limit=56,
    )


def swap(value, axis, bit):
    size = lax.axis_size(axis)
    return lax.ppermute(value, axis, [(i, i ^ bit) for i in range(size)])


def after(value, *others):
    return lax.optimization_barrier((value, *others))[0]


def rows_at(value, start, size):
    return lax.dynamic_slice_in_dim(value, start, size, 0)


def whole(mine, other, bit):
    return jnp.where(
        bit == 0, jnp.concatenate([mine, other], axis=0), jnp.concatenate([other, mine], axis=0)
    )


def place_bit(bit):
    return (lax.axis_index("dp") // bit) % 2


def added(terms, start, size):
    return sum(rows_at(value, offset + start, size).astype(F32) for value, offset in terms)


def deal(value, stride):
    size = lax.axis_size("dp")
    groups = [list(range(first, size, stride)) for first in range(stride)]
    return lax.all_to_all(
        value, "dp", split_axis=0, concat_axis=0, axis_index_groups=groups, tiled=True
    )


def split_high(value):
    high = lax.reduce_precision(value, 8, 7)
    return jnp.concatenate([high.astype(BF16), (value - high).astype(BF16)], axis=0)


def split_exact(value):
    parts = []
    for _ in range(3):
        part = lax.reduce_precision(value, 8, 7)
        parts.append(part.astype(BF16))
        value = value - part
    return jnp.concatenate(parts, axis=0)


class Chain:
    def __init__(self, near, far, route):
        self.near, self.far = [(n, 0) for n in near], [(f, 0) for f in far]
        self.rows = near[0].shape[0]
        self.route = route
        self.value = None
        self.ride = None

    def send(self, *others):
        kind, bit = self.route[0]
        last = self.value if self.value is not None else self.near[-1][0]
        if others:
            last = after(last, *others)
            if self.value is not None:
                self.value = last
            else:
                self.near[-1] = (last, self.near[-1][1])
        if kind == "far":
            out = added(self.far, 0, self.rows).astype(BF16)
            self.sent = swap(out, "tensor", 2)
        elif kind == "sum":
            self.rows //= 2
            self.mine = place_bit(bit)
            start = (1 - self.mine) * self.rows
            parts = [added(self.near, start, self.rows).astype(BF16)]
            if self.far:
                parts.append(added(self.far, start, self.rows).astype(BF16))
            out = jnp.concatenate(parts, axis=0) if len(parts) > 1 else parts[0]
            self.sent = swap(out, "dp", bit)
        elif kind == "part":
            out = added(self.near, 0, self.rows).astype(BF16)
            self.sent = deal(out, bit)
            self.rows //= lax.axis_size("dp") // bit
        elif kind == "gather":
            if self.value is None:
                self.value = added(self.near, 0, self.rows).astype(BF16)
            out = jnp.broadcast_to(self.value[None], (lax.axis_size("dp") // bit, *self.value.shape))
            out = out.reshape(-1, self.value.shape[1])
            self.sent = deal(out, bit)
        else:
            if self.value is None:
                self.value = added(self.near, 0, self.rows).astype(BF16)
            out = self.value
            if self.ride is not None:
                self.ride = split_high(self.ride)
                out = jnp.concatenate([out, self.ride], axis=0)
            self.sent = swap(out, "dp", bit)
        self.out = out
        return out

    def receive(self):
        kind, bit = self.route.pop(0)
        if kind == "far":
            self.near.append((self.sent, 0))
            self.far = []
        elif kind == "sum":
            shift = self.mine * self.rows
            self.near = [(value, offset + shift) for value, offset in self.near] + [(self.sent, 0)]
            if self.far:
                self.far = [(value, offset + shift) for value, offset in self.far]
                self.far.append((self.sent, self.rows))
        elif kind == "part":
            self.near = [(self.sent, j) for j in range(0, self.sent.shape[0], self.rows)]
        elif kind == "gather":
            self.value = self.sent
        else:
            size = self.value.shape[0]
            if self.ride is not None:
                count = self.ride.shape[0] // 2
                other = self.sent[size:]
                self.ride = sum(
                    part[:count].astype(F32) + part[count:].astype(F32) for part in (self.ride, other)
                )
            self.value = whole(self.value, self.sent[:size], place_bit(bit))

    def step(self, *others):
        self.receive()
        if self.route:
            return self.send(*others)
        if others:
            self.value = after(self.value, *others)
        return self.value


def routes():
    bits, size = [], lax.axis_size("dp")
    while 2 ** len(bits) < size:
        bits.append(2 ** len(bits))
    turned = bits[1:] + bits[:1]
    sums = lambda order: [("sum", bit) for bit in order]
    joins = lambda order: [("join", bit) for bit in reversed(order)]
    return sums(bits) + joins(bits), sums(turned) + joins(turned)


def shards(
    patches,
    keep_slots,
    visible_count,
    gain_one,
    shift_one,
    w_qkv,
    b_qv,
    w_out,
    b_out,
    gain_two,
    shift_two,
    w_fc1,
    b_fc1,
    w_fc2,
    b_fc2,
    out_grad,
):
    images, slots = keep_slots.shape
    patch_count, width = patches.shape[1:]
    tensor = lax.axis_size("tensor")
    spot = lax.axis_index("tensor")
    share = images // tensor
    padded = -(-slots // 8) * 8
    part, units = w_qkv.shape[2], w_fc1.shape[1]
    inner = 3 * part
    origin = spot * share
    counts = lax.dynamic_slice_in_dim(visible_count, origin, share, 0)
    keep = lax.dynamic_slice_in_dim(keep_slots, origin, share, 0)
    keep = jnp.pad(keep, ((0, 0), (0, padded - slots)), constant_values=-1)
    patches = lax.dynamic_slice_in_dim(patches, origin, share, 0)
    line = lambda vector: vector.reshape(1, -1)

    bias = jnp.concatenate([b_qv[0], jnp.zeros_like(b_qv[0]), b_qv[1], jnp.zeros_like(b_qv[0])])
    bias = split_exact(line(bias))
    bias = jnp.pad(bias, ((0, 16 - bias.shape[0]), (0, 0)))
    mix = jnp.concatenate([w_qkv.transpose(0, 2, 1).reshape(inner, width), w_out, bias], axis=0)
    far_mix, near_mix = swap(mix, "tensor", 2), swap(mix, "tensor", 1)
    units_biases = [line(b_fc1), swap(line(b_fc1), "tensor", 1)]

    tokens, first, *both = begin(
        counts,
        keep,
        patches,
        out_grad,
        line(gain_one),
        line(shift_one),
        (mix, near_mix),
        inner,
    )
    grad_rows, g_b_fc2, both = both[0], both[1], both[2:]
    three, attended = both[:2], both[2:]
    far_grads = swap(grad_rows, "tensor", 2)
    cross_mix = swap(after(far_mix, first), "tensor", 1)
    mixes = [mix, near_mix, far_mix, cross_mix]
    for r in (2, 3):
        qkv, mixed = attend(counts, after(first, attended[-1]), mixes[r : r + 1], padded, inner)
        three, attended = three + [qkv], attended + [mixed]
    before, seconds = (), []
    for h in range(2):
        middle, second = join(
            tokens,
            attended,
            mixes,
            line(b_out),
            line(gain_two),
            line(shift_two),
            before,
            h,
        )
        before = (middle,)
        seconds.append(second)
    far_seconds = [swap(seconds[0], "tensor", 2)]
    far_seconds.append(swap(seconds[1], "tensor", 2))
    near_up, near_down = (swap(w, "tensor", 1) for w in (w_fc1, w_fc2))
    g_b_fc1, own, far = 0.0, [], []
    total = 2 * first.shape[0]
    *before, mark = unwritten(
        [(total, 2 * units)] * 2 + [(total, width)] * 2, after(seconds[0], seconds[1])
    )
    place_of = lambda number: jnp.full((1,), number, jnp.int32)

    def feeding(place, second, grads, *others):
        nonlocal g_b_fc1, before
        out, back, d_bias, *before = feed(
            after(second, *others),
            grads,
            (w_fc1, near_up),
            (w_fc2, near_down),
            units_biases,
            before,
            place_of(place),
            mark,
        )
        g_b_fc1 += d_bias
        return out, back

    own.append(feeding(0, seconds[0], grad_rows, seconds[1]))
    own.append(feeding(1, seconds[1], grad_rows))
    far.append(feeding(2, after(far_seconds[0], own[1][0]), far_grads))
    backs = [swap(far[0][1], "tensor", 2)]
    mark = swap(far_seconds[0][:8, :128], "tensor", 1)
    far.append(feeding(3, after(far_seconds[1], far[0][0]), far_grads))
    backs.append(swap(far[1][1], "tensor", 2))
    pieces = lax.axis_size("dp")
    units_one = feed_weights(*before, place_of(1), units, pieces)
    near = swap(units_one, "tensor", 1)
    hidden, *rest = before
    units_zero = feed_weights(after(hidden, units_one), *rest, place_of(0), units, pieces)
    first_route, second_route = routes()
    both = Chain([units_zero, near], [], [("sum", 1), ("part", 2), ("gather", 2), ("join", 1)])
    sent = [both.send(units_zero)]
    parts, before = [], ()
    for h in range(2):
        back = after(backs[h], *sent, *before)
        *before, d_gain, d_shift, d_bias = middle_back(
            middle, own[h][1], back, grad_rows, line(gain_two), before, h
        )
        parts.append((d_gain, d_shift, d_bias))
    g_gain_two, g_shift_two, g_b_out = (a + b for a, b in zip(*parts))
    grad_middle, grad_round = before
    mlp = [swap(after(far[h][0], *sent), "tensor", 2) for h in range(2)]

    backward = [None] * 4
    g_b_qkv = [None] * 4

    def attending_back(r, *others):
        backward[r], one, two, g_b_qkv[r] = attend_back(
            counts, after(grad_round, *others), mixes[r], three[r], attended[r], first, padded, 2
        )
        return one, two

    one, two = attending_back(3, *sent)
    far = [swap(one, "tensor", 1), swap(two, "tensor", 1)]
    one, two = attending_back(2)
    sent = [both.step(two)]
    far = jnp.concatenate(
        [
            (a.astype(F32) + after(b, two, *sent).astype(F32)).astype(BF16)
            for a, b in ((one, far[0]), (two, far[1]))
        ]
    )
    sent.append(far)
    far = swap(far, "tensor", 2)
    one, two = attending_back(1, *sent)
    near = [swap(one, "tensor", 1), swap(two, "tensor", 1)]
    one, two = attending_back(0, *mlp)
    ones = Chain([one, near[0], far], [], list(first_route))
    twos = Chain([two, near[1]], [], list(second_route))
    twos.near.append((far, one.shape[0]))
    sent = [ones.send(two), twos.send(two), both.step(two)]
    marks = (swap(both.out[:8, :128], "tensor", 1),)
    grad_patches, g_gain_one, g_shift_one = finish(
        keep,
        after(tokens, *sent),
        backward,
        mixes,
        grad_middle,
        line(gain_one),
        marks,
        patch_count,
        padded,
    )
    shared = jnp.concatenate([g_gain_one, g_shift_one, g_b_out, g_gain_two, g_shift_two, g_b_fc2])
    zero = jnp.zeros((1, units), F32)
    g_b_fc1 = [g_b_fc1[:, :units], g_b_fc1[:, units:], zero, zero]
    local = jnp.concatenate([jnp.concatenate(g_b_qkv), jnp.concatenate(g_b_fc1)], axis=1)
    size = -(-local.shape[1] // width)
    local = jnp.pad(local, ((0, 0), (0, size * width - local.shape[1])))
    local = local.reshape(tensor * size, width)
    small = jnp.concatenate([shared, local], axis=0)
    other = swap(small, "tensor", 1)
    halves = lambda a, b: (a[:6] + b[:6], a[6:].reshape(tensor, size, width), b[6:].reshape(tensor, size, width))
    shared, mine, theirs = halves(small, other)
    pairs = jnp.stack([mine[0] + theirs[1], mine[2] + theirs[3]])
    small = jnp.concatenate([shared, pairs.reshape(2 * size, width)], axis=0)
    other = swap(small, "tensor", 2)
    ride = jnp.concatenate([small[:6] + other[:6], small[6 : 6 + size] + other[6 + size :]], axis=0)
    last = g_shift_one
    while ones.route[1][0] == "sum":
        last = ones.step(last)
        last = twos.step(last)
    last = both.step(last)
    layer_out = close(
        counts,
        middle,
        [o[0] for o in own],
        [after(m, last) for m in mlp],
        line(b_fc2),
        padded,
        slots,
    )
    twos.ride = ride
    while ones.route:
        last = ones.step(last)
        last = twos.step(last)
    last = both.step(last)
    ride = twos.ride
    both = both.value.reshape(pieces, 2, units // pieces, width).astype(F32)
    grad_w_fc1, grad_w_fc2 = (both[:, j].reshape(units, width) for j in range(2))
    qk, vo = ones.value.astype(F32), twos.value.astype(F32)
    local = ride[6:].reshape(1, -1)[0]
    shared = ride[:6]
    grad_w_qkv = jnp.concatenate([qk, vo[:part]], axis=0).reshape(3, part, width).transpose(0, 2, 1)
    grad_b_qv = jnp.stack([local[:part], local[2 * part : inner]])
    return (
        layer_out,
        grad_patches,
        shared[0],
        shared[1],
        grad_w_qkv,
        grad_b_qv,
        vo[part:],
        shared[2],
        shared[3],
        shared[4],
        grad_w_fc1,
        local[inner : inner + units],
        grad_w_fc2,
        shared[5],
    )


def solution(mesh):
    return jax.shard_map(
        shards,
        mesh=mesh,
        in_specs=(
            P("dp", None, None),
            P("dp", None),
            P("dp"),
            P(),
            P(),
            P(None, None, "tensor"),
            P(None, "tensor"),
            P("tensor", None),
            P(),
            P(),
            P(),
            P(None, "tensor"),
            P("tensor"),
            P("tensor", None),
            P(),
            P(("dp", "tensor"), None, None),
        ),
        out_specs=(
            P(("dp", "tensor"), None, None),
            P(("dp", "tensor"), None, None),
            P(),
            P(),
            P(None, None, "tensor"),
            P(None, "tensor"),
            P("tensor", None),
            P(),
            P(),
            P(),
            P(None, "tensor"),
            P("tensor"),
            P("tensor", None),
            P(),
        ),
        check_vma=False,
    )
```

```python
import functools

import jax
import jax.numpy as jnp
from jax import lax
from jax.experimental import pallas as pl
from jax.experimental.pallas import tpu as pltpu
from jax.sharding import PartitionSpec as P

HD = 64
EPSILON = 1e-06
MASKED = -1000000000.0
F32 = jnp.float32
BF16 = jnp.bfloat16
VMEM = pltpu.VMEM
NN = (((1,), (0,)), ((), ()))
NT = (((1,), (1,)), ((), ()))
TN = (((0,), (0,)), ((), ()))


def dot(left, right, dims=NN):
    return lax.dot_general(left, right, dims, preferred_element_type=F32)


def standard(inputs):
    average = jnp.mean(inputs, axis=-1, keepdims=True)
    centered = inputs - average
    spread = jnp.mean(centered * centered, axis=-1, keepdims=True)
    inverse = lax.rsqrt(spread + EPSILON)
    return centered * inverse, inverse


def norm_back(normal, inverse, gain, gradient):
    scaled = gradient * gain
    first = jnp.mean(scaled, axis=-1, keepdims=True)
    second = jnp.mean(scaled * normal, axis=-1, keepdims=True)
    return inverse * (scaled - first - normal * second)


def slots_matrix(keep_row, patch_count):
    places = lax.broadcasted_iota(jnp.int32, (patch_count, keep_row.shape[1]), 0)
    return (places == keep_row).astype(F32).astype(BF16)


def add_row(ref, value):
    row = jnp.sum(value, axis=0, keepdims=True)

    @pl.when(pl.program_id(0) == 0)
    def _():
        ref[...] = jnp.zeros_like(ref)

    ref[...] += row


def full(shape):
    return pl.BlockSpec(shape, lambda i, *_: (0,) * len(shape))


def rows(count, width):
    return pl.BlockSpec((count, width), lambda i, *_: (i, 0))


def call(body, grid, scalars, ins, in_specs, outs, out_specs, scratch=(), flops=0, alias=None, limit=24):
    size = sum(a.size * a.dtype.itemsize for a in ins)
    size += sum(o.size * o.dtype.itemsize for o in outs)
    return pl.pallas_call(
        body,
        out_shape=outs,
        grid_spec=pltpu.PrefetchScalarGridSpec(
            num_scalar_prefetch=len(scalars),
            grid=grid,
            in_specs=in_specs,
            out_specs=out_specs,
            scratch_shapes=scratch,
        ),
        compiler_params=pltpu.CompilerParams(vmem_limit_bytes=limit * 2**20),
        input_output_aliases=alias or {},
        cost_estimate=pl.CostEstimate(flops=100 * flops, bytes_accessed=100 * size, transcendentals=0),
    )(*scalars, *ins)


def shape_of(shape, kind):
    return jax.ShapeDtypeStruct(shape, kind)


def heads_of(width):
    lanes = lax.broadcasted_iota(jnp.int32, (1, width), 1) // HD
    return [(lanes == h).astype(BF16) for h in range(width // HD)]


def stacked(values, masks):
    return jnp.concatenate([values * m for m in masks], axis=0)


def merged(values, masks, length):
    lanes = lax.broadcasted_iota(jnp.int32, (1, values.shape[1]), 1) // HD
    result = values[0:length]
    for h in range(1, len(masks)):
        result = jnp.where(lanes == h, values[h * length : (h + 1) * length], result)
    return result


def probabilities(queries, keys, count, masks):
    scores = dot(stacked(queries, masks), keys, NT) * HD**-0.5
    seen = lax.broadcasted_iota(jnp.int32, (1, keys.shape[0]), 1) < count
    scores = jnp.where(seen, scores, MASKED)
    powers = jnp.exp(scores - jnp.max(scores, axis=-1, keepdims=True))
    return powers / jnp.sum(powers, axis=-1, keepdims=True)


def attention(first, w_ref, counts, masks, qkv_ref, out_ref, padded):
    inner = qkv_ref.shape[1]
    part = inner // 3
    bias = jnp.sum(w_ref[inner + part :, :].astype(F32), axis=0, keepdims=True)[:, :inner]
    qkv = (dot(first, w_ref[:inner, :], NT) + bias).astype(BF16)
    qkv_ref[...] = qkv
    for g, count in enumerate(counts):
        here = slice(g * padded, (g + 1) * padded)
        q, k, v = (qkv[here, j * part : (j + 1) * part] for j in range(3))
        chances = probabilities(q, k, count, masks).astype(BF16)
        out_ref[here, :] = merged(dot(chances, v), masks, padded).astype(BF16)


def begin(counts, keep, patches, out_grad, gain, shift, weights, inner):
    share, padded = keep.shape
    slots = out_grad.shape[1]
    patch_count, width = patches.shape[1:]
    total, n = share * padded, len(weights)
    part = inner // 3
    group = 2
    size = group * padded

    def body(count_ref, keep_ref, patch_ref, grad_ref, gain_ref, shift_ref, *refs):
        w_refs, outs = refs[:n], refs[n:]
        tokens_ref, first_ref, rows_ref, sum_ref = outs[:4]
        qkv_refs, att_refs = outs[4 : 4 + n], outs[4 + n :]
        masks = heads_of(part)
        total_sum = jnp.zeros((1, width), F32)
        for g in range(group):
            image = pl.program_id(0) * group + g
            here = slice(g * padded, (g + 1) * padded)
            picks = slots_matrix(keep_ref[pl.ds(image, 1), :], patch_count)
            tokens = dot(picks, patch_ref[g], TN)
            tokens_ref[here, :] = tokens.astype(BF16)
            normal, _ = standard(tokens)
            first = (normal * gain_ref[...] + shift_ref[...]).astype(BF16)
            first_ref[here, :] = first
            seen = lax.broadcasted_iota(jnp.int32, (slots, 1), 0) < count_ref[image]
            grads = jnp.where(seen, grad_ref[g].astype(F32), 0.0)
            rows_ref[here, :] = jnp.zeros((padded, width), BF16)
            rows_ref[g * padded : g * padded + slots, :] = grads.astype(BF16)
            total_sum += jnp.sum(grads, axis=0, keepdims=True)
        counts = [count_ref[pl.program_id(0) * group + g] for g in range(group)]
        for w_ref, qkv_ref, att_ref in zip(w_refs, qkv_refs, att_refs):
            attention(first_ref[...], w_ref, counts, masks, qkv_ref, att_ref, padded)
        add_row(sum_ref, total_sum)

    return call(
        body,
        (share // group,),
        (counts,),
        (keep, patches, out_grad, gain, shift, *weights),
        [
            full(keep.shape),
            pl.BlockSpec((group, patch_count, width), lambda i, *_: (i, 0, 0)),
            pl.BlockSpec((group, slots, width), lambda i, *_: (i, 0, 0)),
            full(gain.shape),
            full(shift.shape),
        ]
        + [full(w.shape) for w in weights],
        (shape_of((total, width), BF16),) * 3
        + (shape_of((1, width), F32),)
        + (shape_of((total, inner), BF16),) * n
        + (shape_of((total, part), BF16),) * n,
        [rows(size, width)] * 3
        + [full((1, width))]
        + [rows(size, inner)] * n
        + [rows(size, part)] * n,
        flops=2 * total * (patch_count + n * inner) * width,
    )


def attend(counts, first, weights, padded, inner):
    total, width = first.shape
    n, part = len(weights), inner // 3
    group = 2
    size = group * padded

    def body(count_ref, first_ref, *refs):
        w_refs, qkv_refs, att_refs = refs[:n], refs[n : 2 * n], refs[2 * n :]
        masks = heads_of(part)
        counts = [count_ref[pl.program_id(0) * group + g] for g in range(group)]
        for w_ref, qkv_ref, att_ref in zip(w_refs, qkv_refs, att_refs):
            attention(first_ref[...], w_ref, counts, masks, qkv_ref, att_ref, padded)

    return call(
        body,
        (total // size,),
        (counts,),
        (first, *weights),
        [rows(size, width)] + [full(w.shape) for w in weights],
        (shape_of((total, inner), BF16),) * n + (shape_of((total, part), BF16),) * n,
        [rows(size, inner)] * n + [rows(size, part)] * n,
        flops=2 * total * n * inner * width,
    )


def join(tokens, attended, w_outs, b_out, gain, shift, before, h):
    total, width = tokens.shape
    size, n = total // 2, len(attended)
    part = attended[0].shape[1]

    def body(tokens_ref, *refs):
        att_refs, o_refs, refs = refs[:n], refs[n : 2 * n], refs[2 * n :]
        bias_ref, gain_ref, shift_ref = refs[:3]
        middle_ref, second_ref = refs[3 + len(before) :]
        rows_of_out = slice(3 * part, 4 * part)
        branch = sum(dot(a[...], o[rows_of_out, :]) for a, o in zip(att_refs, o_refs))
        middle = tokens_ref[...].astype(F32) + branch + bias_ref[...]
        middle_ref[...] = middle
        normal, _ = standard(middle)
        second_ref[...] = (normal * gain_ref[...] + shift_ref[...]).astype(BF16)

    at = lambda wide: pl.BlockSpec((size, wide), lambda i: (h, 0))
    ins = (tokens, *attended, *w_outs, b_out, gain, shift)
    specs = [at(width)] + [at(part)] * n + [full(w.shape) for w in ins[1 + n :]]
    return call(
        body,
        (1,),
        (),
        ins + tuple(before),
        specs + [pl.BlockSpec(memory_space=pl.ANY)] * len(before),
        (shape_of((total, width), F32), shape_of((size, width), BF16)),
        [at(width), full((size, width))],
        flops=2 * size * width * width,
        alias={len(ins) + j: j for j in range(len(before))},
    )


def unwritten(shapes, first):
    def body(first_ref, *refs):
        refs[-1][...] = jnp.zeros_like(refs[-1])

    outs = (*(shape_of(shape, BF16) for shape in shapes), shape_of((8, 128), BF16))
    return pl.pallas_call(
        body,
        out_shape=outs,
        in_specs=[pl.BlockSpec(memory_space=pl.ANY)],
        out_specs=[pl.BlockSpec(memory_space=pl.ANY)] * len(shapes) + [pl.BlockSpec(memory_space=pltpu.VMEM)],
        compiler_params=pltpu.CompilerParams(vmem_limit_bytes=2**20),
    )(first)


def feed(second, grads, ups, downs, biases, before, place, mark):
    size, width = second.shape
    n, units = len(ups), ups[0].shape[1]
    root = 0.5**0.5
    density = (2.0 * jnp.pi) ** -0.5

    def body(place_ref, *refs):
        second_ref, grads_ref = refs[:2]
        up_refs, down_refs, bias_refs = (refs[2 + j * n : 2 + (j + 1) * n] for j in range(3))
        out_ref, back_ref, d_bias_ref, hidden_ref, inner_ref, rows_ref, grad_rows_ref = refs[
            2 + 3 * n + len(before) + 1 :
        ]
        rows_ref[...] = second_ref[...]
        grad_rows_ref[...] = grads_ref[...]
        out = back = 0.0
        for j in range(n):
            cols = slice(j * units, (j + 1) * units)
            u = dot(second_ref[...], up_refs[j][...]) + bias_refs[j][...]
            gh = dot(grads_ref[...], down_refs[j][...], NT)
            below = 0.5 + 0.5 * lax.erf(u * root)
            hidden = (u * below).astype(BF16)
            slope = below + u * (jnp.exp(-0.5 * u * u) * density)
            gi = (gh * slope).astype(BF16)
            hidden_ref[:, cols] = hidden
            inner_ref[:, cols] = gi
            d_bias_ref[:, cols] = jnp.sum(gi.astype(F32), axis=0, keepdims=True)
            out += dot(hidden, down_refs[j][...])
            back += dot(gi, up_refs[j][...], NT)
        out_ref[...] = out.astype(BF16)
        back_ref[...] = back.astype(BF16)

    ins = (second, grads, *ups, *downs, *biases)
    specs = [full(a.shape) for a in ins]
    specs[1] = pl.BlockSpec((size, width), lambda i, p: (p[0] % 2, 0))
    at = lambda wide: pl.BlockSpec((size, wide), lambda i, p: (p[0], 0))
    outs = (
        shape_of((size, width), BF16),
        shape_of((size, width), BF16),
        shape_of((1, n * units), F32),
        *(shape_of(a.shape, a.dtype) for a in before),
    )
    return call(
        body,
        (1,),
        (place,),
        ins + tuple(before) + (mark,),
        specs + [pl.BlockSpec(memory_space=pl.ANY)] * (len(before) + 1),
        outs,
        [full(o.shape) for o in outs[:3]] + [at(n * units)] * 2 + [at(width)] * 2,
        flops=8 * size * width * n * units,
        alias={1 + len(ins) + j: 3 + j for j in range(len(before))},
        limit=32,
    )


def feed_weights(hidden, inner, second, grads, j, width, pieces):
    total = second.shape[0]
    wide = second.shape[1]
    size = width // pieces

    def body(place_ref, hidden_ref, inner_ref, second_ref, grads_ref, out_ref):
        up = dot(second_ref[...], inner_ref[...], TN).astype(BF16)
        for p in range(pieces):
            out_ref[2 * p * size : (2 * p + 1) * size, :] = up[p * size : (p + 1) * size]
        down = dot(hidden_ref[...], grads_ref[...], TN).astype(BF16)
        for p in range(pieces):
            out_ref[(2 * p + 1) * size : (2 * p + 2) * size, :] = down[p * size : (p + 1) * size]

    at = pl.BlockSpec((total, width), lambda i, p: (0, p[0]))
    return call(
        body,
        (1,),
        (j,),
        (hidden, inner, second, grads),
        [at, at, full(second.shape), full(grads.shape)],
        (shape_of((2 * width, wide), BF16),),
        [full((2 * width, wide))],
        flops=4 * total * width * wide,
        limit=32,
    )[0]


def middle_back(middle, back, back_far, grads, gain, before, h):
    total, width = middle.shape
    size = total // 2

    def body(middle_ref, back_ref, far_ref, grads_ref, gain_ref, *refs):
        grad_ref, round_ref, d_gain_ref, d_shift_ref, d_bias_ref = refs[len(before) :]
        back = back_ref[...].astype(F32) + far_ref[...].astype(F32)
        normal, inverse = standard(middle_ref[...])
        grad = grads_ref[...].astype(F32) + norm_back(normal, inverse, gain_ref[...], back)
        grad_ref[...] = grad
        round_ref[...] = grad.astype(BF16)
        for ref, value in ((d_gain_ref, back * normal), (d_shift_ref, back), (d_bias_ref, grad)):
            ref[...] = jnp.sum(value, axis=0, keepdims=True)

    at = pl.BlockSpec((size, width), lambda i: (h, 0))
    one = shape_of((1, width), F32)
    return call(
        body,
        (1,),
        (),
        (middle, back, back_far, grads, gain, *before),
        [at, full((size, width)), full((size, width)), at, full((1, width))]
        + [pl.BlockSpec(memory_space=pl.ANY)] * len(before),
        (shape_of((total, width), F32), shape_of((total, width), BF16), one, one, one),
        [at, at] + [full((1, width))] * 3,
        flops=10 * total * width,
        alias={5 + j: j for j in range(len(before))},
    )


def attend_back(counts, grad, weights, qkv, attended, first, padded, group):
    total, width = grad.shape
    inner, part = qkv.shape[1], attended.shape[1]
    share = total // padded
    steps, size = share // group, group * padded
    cut = 2 * part

    def body(count_ref, grad_ref, first_ref, w_ref, qkv_ref, att_ref, three_ref, one_ref, two_ref, bias_ref):
        step = pl.program_id(0)
        masks = heads_of(part)
        base = pl.multiple_of(step * size, size)
        w_out = w_ref[inner : inner + part, :]
        ga_group = dot(grad_ref[pl.ds(base, size), :], w_out, NT).astype(BF16)
        for i in range(group):
            where = pl.ds(base + i * padded, padded)
            here = slice(i * padded, (i + 1) * padded)
            count = count_ref[step * group + i]
            ga = ga_group[here]
            q, k, v = (qkv_ref[here, j * part : (j + 1) * part] for j in range(3))
            exact = probabilities(q, k, count, masks)
            ga_all = stacked(ga, masks)
            gp = dot(ga_all, v, NT)
            gs = exact * (gp - jnp.sum(exact * gp, axis=-1, keepdims=True))
            gs = gs.astype(BF16)
            gq = merged(dot(gs, k), masks, padded) * HD**-0.5
            gk = dot(gs, stacked(q, masks), TN) * HD**-0.5
            gv = dot(exact.astype(BF16), ga_all, TN)
            three_ref[where, :] = jnp.concatenate([x.astype(BF16) for x in (gq, gk, gv)], axis=1)

        @pl.when(step == steps - 1)
        def _():
            one_ref[...] = dot(three_ref[:, :cut], first_ref[...], TN).astype(BF16)
            two_ref[: inner - cut, :] = dot(three_ref[:, cut:], first_ref[...], TN).astype(BF16)
            two_ref[inner - cut :, :] = dot(att_ref[...], grad_ref[...], TN).astype(BF16)
            bias_ref[...] = jnp.sum(three_ref[...].astype(F32), axis=0, keepdims=True)

    ins = (grad, first, weights, qkv, attended)
    specs = [full(a.shape) for a in ins]
    specs[3] = rows(size, inner)
    outs = (
        shape_of((total, inner), BF16),
        shape_of((cut, width), BF16),
        shape_of((inner - cut + part, width), BF16),
        shape_of((1, inner), F32),
    )
    return call(
        body,
        (steps,),
        (counts,),
        ins,
        specs,
        outs,
        [full(o.shape) for o in outs],
        flops=5 * total * width * width,
        limit=36,
    )


def close(counts, middle, outs, outs_far, b_fc2, padded, slots):
    total, width = middle.shape
    share = total // padded
    half = share // 2

    def body(count_ref, middle_ref, *refs):
        out_refs, far_refs, bias_ref, layer_ref = refs[:2], refs[2:4], refs[4], refs[5]
        for i in range(share):
            h, here = i // half, slice(i % half * padded, (i % half + 1) * padded)
            layer = middle_ref[i * padded : (i + 1) * padded, :] + bias_ref[...]
            layer = layer + (out_refs[h][here, :].astype(F32) + far_refs[h][here, :].astype(F32))
            seen = lax.broadcasted_iota(jnp.int32, (padded, 1), 0) < count_ref[i]
            layer_ref[i] = jnp.where(seen, layer, 0.0).astype(BF16)[0:slots]

    ins = (middle, *outs, *outs_far, b_fc2)
    shape = (share, slots, width)
    return call(
        body,
        (1,),
        (counts,),
        ins,
        [full(a.shape) for a in ins],
        (shape_of(shape, BF16),),
        [full(shape)],
        flops=4 * total * width,
    )[0]


def finish(keep, tokens, threes, weights, grad, gain, marks, patch_count, padded):
    total, width = tokens.shape
    share, n, inner = total // padded, len(threes), threes[0].shape[1]
    group = share // 2
    size = group * padded

    def body(keep_ref, tokens_ref, grad_ref, gain_ref, *refs):
        three_refs, w_refs = refs[:n], refs[n : 2 * n]
        out_ref, d_gain_ref, d_shift_ref = refs[2 * n + len(marks) :]
        back = sum(dot(t[...], w[:inner, :]) for t, w in zip(three_refs, w_refs))
        normal, inverse = standard(tokens_ref[...].astype(F32))
        grad = grad_ref[...] + norm_back(normal, inverse, gain_ref[...], back)
        add_row(d_gain_ref, back * normal)
        add_row(d_shift_ref, back)
        high = grad.astype(BF16)
        low = (grad - high.astype(F32)).astype(BF16)
        for g in range(group):
            here = slice(g * padded, (g + 1) * padded)
            image = pl.program_id(0) * group + g
            picks = slots_matrix(keep_ref[pl.ds(image, 1), :], patch_count)
            out_ref[g] = dot(picks, high[here]) + dot(picks, low[here])

    one = shape_of((1, width), F32)
    return call(
        body,
        (2,),
        (),
        (keep, tokens, grad, gain, *threes, *weights, *marks),
        [full(keep.shape), rows(size, width), rows(size, width), full((1, width))]
        + [rows(size, inner)] * n
        + [full(w.shape) for w in weights]
        + [pl.BlockSpec(memory_space=pl.ANY)] * len(marks),
        (shape_of((share, patch_count, width), F32), one, one),
        [pl.BlockSpec((group, patch_count, width), lambda i, *_: (i, 0, 0))] + [full((1, width))] * 2,
        flops=2 * total * (n * inner + 2 * patch_count) * width,
        limit=56,
    )


def swap(value, axis, bit):
    size = lax.axis_size(axis)
    return lax.ppermute(value, axis, [(i, i ^ bit) for i in range(size)])


def after(value, *others):
    return lax.optimization_barrier((value, *others))[0]


def rows_at(value, start, size):
    return lax.dynamic_slice_in_dim(value, start, size, 0)


def whole(mine, other, bit):
    return jnp.where(
        bit == 0, jnp.concatenate([mine, other], axis=0), jnp.concatenate([other, mine], axis=0)
    )


def place_bit(bit):
    return (lax.axis_index("dp") // bit) % 2


def added(terms, start, size):
    return sum(rows_at(value, offset + start, size).astype(F32) for value, offset in terms)


def deal(value, stride):
    size = lax.axis_size("dp")
    groups = [list(range(first, size, stride)) for first in range(stride)]
    return lax.all_to_all(
        value, "dp", split_axis=0, concat_axis=0, axis_index_groups=groups, tiled=True
    )


def split_high(value):
    high = lax.reduce_precision(value, 8, 7)
    return jnp.concatenate([high.astype(BF16), (value - high).astype(BF16)], axis=0)


def split_exact(value):
    parts = []
    for _ in range(3):
        part = lax.reduce_precision(value, 8, 7)
        parts.append(part.astype(BF16))
        value = value - part
    return jnp.concatenate(parts, axis=0)


class Chain:
    def __init__(self, near, far, route):
        self.near, self.far = [(n, 0) for n in near], [(f, 0) for f in far]
        self.rows = near[0].shape[0]
        self.route = route
        self.value = None
        self.ride = None

    def send(self, *others):
        kind, bit = self.route[0]
        last = self.value if self.value is not None else self.near[-1][0]
        if others:
            last = after(last, *others)
            if self.value is not None:
                self.value = last
            else:
                self.near[-1] = (last, self.near[-1][1])
        if kind == "far":
            out = added(self.far, 0, self.rows).astype(BF16)
            self.sent = swap(out, "tensor", 2)
        elif kind == "sum":
            self.rows //= 2
            self.mine = place_bit(bit)
            start = (1 - self.mine) * self.rows
            parts = [added(self.near, start, self.rows).astype(BF16)]
            if self.far:
                parts.append(added(self.far, start, self.rows).astype(BF16))
            out = jnp.concatenate(parts, axis=0) if len(parts) > 1 else parts[0]
            self.sent = swap(out, "dp", bit)
        elif kind == "part":
            out = added(self.near, 0, self.rows).astype(BF16)
            self.sent = deal(out, bit)
            self.rows //= lax.axis_size("dp") // bit
        elif kind == "gather":
            if self.value is None:
                self.value = added(self.near, 0, self.rows).astype(BF16)
            out = jnp.broadcast_to(self.value[None], (lax.axis_size("dp") // bit, *self.value.shape))
            out = out.reshape(-1, self.value.shape[1])
            self.sent = deal(out, bit)
        else:
            if self.value is None:
                self.value = added(self.near, 0, self.rows).astype(BF16)
            out = self.value
            if self.ride is not None:
                self.ride = split_high(self.ride)
                out = jnp.concatenate([out, self.ride], axis=0)
            self.sent = swap(out, "dp", bit)
        self.out = out
        return out

    def receive(self):
        kind, bit = self.route.pop(0)
        if kind == "far":
            self.near.append((self.sent, 0))
            self.far = []
        elif kind == "sum":
            shift = self.mine * self.rows
            self.near = [(value, offset + shift) for value, offset in self.near] + [(self.sent, 0)]
            if self.far:
                self.far = [(value, offset + shift) for value, offset in self.far]
                self.far.append((self.sent, self.rows))
        elif kind == "part":
            self.near = [(self.sent, j) for j in range(0, self.sent.shape[0], self.rows)]
        elif kind == "gather":
            self.value = self.sent
        else:
            size = self.value.shape[0]
            if self.ride is not None:
                count = self.ride.shape[0] // 2
                other = self.sent[size:]
                self.ride = sum(
                    part[:count].astype(F32) + part[count:].astype(F32) for part in (self.ride, other)
                )
            self.value = whole(self.value, self.sent[:size], place_bit(bit))

    def step(self, *others):
        self.receive()
        if self.route:
            return self.send(*others)
        if others:
            self.value = after(self.value, *others)
        return self.value


def routes():
    bits, size = [], lax.axis_size("dp")
    while 2 ** len(bits) < size:
        bits.append(2 ** len(bits))
    turned = bits[1:] + bits[:1]
    sums = lambda order: [("sum", bit) for bit in order]
    joins = lambda order: [("join", bit) for bit in reversed(order)]
    return sums(bits) + joins(bits), sums(turned) + joins(turned)


def shards(
    patches,
    keep_slots,
    visible_count,
    gain_one,
    shift_one,
    w_qkv,
    b_qv,
    w_out,
    b_out,
    gain_two,
    shift_two,
    w_fc1,
    b_fc1,
    w_fc2,
    b_fc2,
    out_grad,
):
    images, slots = keep_slots.shape
    patch_count, width = patches.shape[1:]
    tensor = lax.axis_size("tensor")
    spot = lax.axis_index("tensor")
    share = images // tensor
    padded = -(-slots // 8) * 8
    part, units = w_qkv.shape[2], w_fc1.shape[1]
    inner = 3 * part
    origin = spot * share
    counts = lax.dynamic_slice_in_dim(visible_count, origin, share, 0)
    keep = lax.dynamic_slice_in_dim(keep_slots, origin, share, 0)
    keep = jnp.pad(keep, ((0, 0), (0, padded - slots)), constant_values=-1)
    patches = lax.dynamic_slice_in_dim(patches, origin, share, 0)
    line = lambda vector: vector.reshape(1, -1)

    bias = jnp.concatenate([b_qv[0], jnp.zeros_like(b_qv[0]), b_qv[1], jnp.zeros_like(b_qv[0])])
    bias = split_exact(line(bias))
    bias = jnp.pad(bias, ((0, 16 - bias.shape[0]), (0, 0)))
    mix = jnp.concatenate([w_qkv.transpose(0, 2, 1).reshape(inner, width), w_out, bias], axis=0)
    far_mix, near_mix = swap(mix, "tensor", 2), swap(mix, "tensor", 1)
    units_biases = [line(b_fc1), swap(line(b_fc1), "tensor", 1)]

    tokens, first, *both = begin(
        counts,
        keep,
        patches,
        out_grad,
        line(gain_one),
        line(shift_one),
        (mix, near_mix),
        inner,
    )
    grad_rows, g_b_fc2, both = both[0], both[1], both[2:]
    three, attended = both[:2], both[2:]
    far_grads = swap(grad_rows, "tensor", 2)
    cross_mix = swap(after(far_mix, first), "tensor", 1)
    mixes = [mix, near_mix, far_mix, cross_mix]
    for r in (2, 3):
        qkv, mixed = attend(counts, after(first, attended[-1]), mixes[r : r + 1], padded, inner)
        three, attended = three + [qkv], attended + [mixed]
    before, seconds = (), []
    for h in range(2):
        middle, second = join(
            tokens,
            attended,
            mixes,
            line(b_out),
            line(gain_two),
            line(shift_two),
            before,
            h,
        )
        before = (middle,)
        seconds.append(second)
    far_seconds = [swap(seconds[0], "tensor", 2)]
    far_seconds.append(swap(seconds[1], "tensor", 2))
    near_up, near_down = (swap(w, "tensor", 1) for w in (w_fc1, w_fc2))
    g_b_fc1, own, far = 0.0, [], []
    total = 2 * first.shape[0]
    *before, mark = unwritten(
        [(total, 2 * units)] * 2 + [(total, width)] * 2, after(seconds[0], seconds[1])
    )
    place_of = lambda number: jnp.full((1,), number, jnp.int32)

    def feeding(place, second, grads, *others):
        nonlocal g_b_fc1, before
        out, back, d_bias, *before = feed(
            after(second, *others),
            grads,
            (w_fc1, near_up),
            (w_fc2, near_down),
            units_biases,
            before,
            place_of(place),
            mark,
        )
        g_b_fc1 += d_bias
        return out, back

    own.append(feeding(0, seconds[0], grad_rows, seconds[1]))
    own.append(feeding(1, seconds[1], grad_rows))
    far.append(feeding(2, after(far_seconds[0], own[1][0]), far_grads))
    backs = [swap(far[0][1], "tensor", 2)]
    mark = swap(far_seconds[0][:8, :128], "tensor", 1)
    far.append(feeding(3, after(far_seconds[1], far[0][0]), far_grads))
    backs.append(swap(far[1][1], "tensor", 2))
    pieces = lax.axis_size("dp")
    units_one = feed_weights(*before, place_of(1), units, pieces)
    near = swap(units_one, "tensor", 1)
    hidden, *rest = before
    units_zero = feed_weights(after(hidden, units_one), *rest, place_of(0), units, pieces)
    first_route, second_route = routes()
    both = Chain([units_zero, near], [], [("sum", 1), ("part", 2), ("gather", 2), ("join", 1)])
    sent = [both.send(units_zero)]
    parts, before = [], ()
    for h in range(2):
        back = after(backs[h], *sent, *before)
        *before, d_gain, d_shift, d_bias = middle_back(
            middle, own[h][1], back, grad_rows, line(gain_two), before, h
        )
        parts.append((d_gain, d_shift, d_bias))
    g_gain_two, g_shift_two, g_b_out = (a + b for a, b in zip(*parts))
    grad_middle, grad_round = before
    mlp = [swap(after(far[h][0], *sent), "tensor", 2) for h in range(2)]

    backward = [None] * 4
    g_b_qkv = [None] * 4

    def attending_back(r, *others):
        backward[r], one, two, g_b_qkv[r] = attend_back(
            counts, after(grad_round, *others), mixes[r], three[r], attended[r], first, padded, 2
        )
        return one, two

    one, two = attending_back(3, *sent)
    far = [swap(one, "tensor", 1), swap(two, "tensor", 1)]
    one, two = attending_back(2)
    sent = [both.step(two)]
    far = jnp.concatenate(
        [
            (a.astype(F32) + after(b, two, *sent).astype(F32)).astype(BF16)
            for a, b in ((one, far[0]), (two, far[1]))
        ]
    )
    sent.append(far)
    far = swap(far, "tensor", 2)
    one, two = attending_back(1, *sent)
    near = [swap(one, "tensor", 1), swap(two, "tensor", 1)]
    one, two = attending_back(0, *mlp)
    ones = Chain([one, near[0], far], [], list(first_route))
    twos = Chain([two, near[1]], [], list(second_route))
    twos.near.append((far, one.shape[0]))
    sent = [ones.send(two), twos.send(two), both.step(two)]
    marks = (swap(both.out[:8, :128], "tensor", 1),)
    grad_patches, g_gain_one, g_shift_one = finish(
        keep,
        after(tokens, *sent),
        backward,
        mixes,
        grad_middle,
        line(gain_one),
        marks,
        patch_count,
        padded,
    )
    shared = jnp.concatenate([g_gain_one, g_shift_one, g_b_out, g_gain_two, g_shift_two, g_b_fc2])
    zero = jnp.zeros((1, units), F32)
    g_b_fc1 = [g_b_fc1[:, :units], g_b_fc1[:, units:], zero, zero]
    local = jnp.concatenate([jnp.concatenate(g_b_qkv), jnp.concatenate(g_b_fc1)], axis=1)
    size = -(-local.shape[1] // width)
    local = jnp.pad(local, ((0, 0), (0, size * width - local.shape[1])))
    local = local.reshape(tensor * size, width)
    small = jnp.concatenate([shared, local], axis=0)
    other = swap(small, "tensor", 1)
    halves = lambda a, b: (a[:6] + b[:6], a[6:].reshape(tensor, size, width), b[6:].reshape(tensor, size, width))
    shared, mine, theirs = halves(small, other)
    pairs = jnp.stack([mine[0] + theirs[1], mine[2] + theirs[3]])
    small = jnp.concatenate([shared, pairs.reshape(2 * size, width)], axis=0)
    other = swap(small, "tensor", 2)
    ride = jnp.concatenate([small[:6] + other[:6], small[6 : 6 + size] + other[6 + size :]], axis=0)
    last = g_shift_one
    while ones.route[1][0] == "sum":
        last = ones.step(last)
        last = twos.step(last)
    last = both.step(last)
    layer_out = close(
        counts,
        middle,
        [o[0] for o in own],
        [after(m, last) for m in mlp],
        line(b_fc2),
        padded,
        slots,
    )
    twos.ride = ride
    while ones.route:
        last = ones.step(last)
        last = twos.step(last)
    mine, theirs = (
        v.reshape(pieces // 2, 2, units // pieces, width) for v in (both.value, after(both.sent, last))
    )
    ride = twos.ride
    grad_w_fc1, grad_w_fc2 = (
        whole(mine[:, j].reshape(-1, width), theirs[:, j].reshape(-1, width), place_bit(1)).astype(F32)
        for j in range(2)
    )
    qk, vo = ones.value.astype(F32), twos.value.astype(F32)
    local = ride[6:].reshape(1, -1)[0]
    shared = ride[:6]
    grad_w_qkv = jnp.concatenate([qk, vo[:part]], axis=0).reshape(3, part, width).transpose(0, 2, 1)
    grad_b_qv = jnp.stack([local[:part], local[2 * part : inner]])
    return (
        layer_out,
        grad_patches,
        shared[0],
        shared[1],
        grad_w_qkv,
        grad_b_qv,
        vo[part:],
        shared[2],
        shared[3],
        shared[4],
        grad_w_fc1,
        local[inner : inner + units],
        grad_w_fc2,
        shared[5],
    )


def solution(mesh):
    return jax.shard_map(
        shards,
        mesh=mesh,
        in_specs=(
            P("dp", None, None),
            P("dp", None),
            P("dp"),
            P(),
            P(),
            P(None, None, "tensor"),
            P(None, "tensor"),
            P("tensor", None),
            P(),
            P(),
            P(),
            P(None, "tensor"),
            P("tensor"),
            P("tensor", None),
            P(),
            P(("dp", "tensor"), None, None),
        ),
        out_specs=(
            P(("dp", "tensor"), None, None),
            P(("dp", "tensor"), None, None),
            P(),
            P(),
            P(None, None, "tensor"),
            P(None, "tensor"),
            P("tensor", None),
            P(),
            P(),
            P(),
            P(None, "tensor"),
            P("tensor"),
            P("tensor", None),
            P(),
        ),
        check_vma=False,
    )
```
